1024 devices in a mesh: section: 64 (over x, z), head: 16 (over y, core).
Axes of the slice: x: 8, y: 8, z: 8, core: 2. Of those that a mesh axis runs over, the one named last changes fastest.
Arguments:
- entering: bfloat16 [64, 128, 4096], P('section', None, 'head'), may hold values from -6 to 6, as said below
- fresh_slice: bfloat16 [128, 4096], P(None, 'head'), may hold values from -6 to 6
- norm_gain: float32 [64, 4096], P('section'), may hold values from 0.5 to 1.5
- w_query: bfloat16 [64, 4096, 4096], P('section', None, 'head'), may hold values from -18.8125 to 18.8125
- w_key_value: bfloat16 [64, 4096, 1024], P('section', None, 'head'), may hold values from -0.0625 to 0.0625
- doc_lengths: int32 [65], replicated, may hold values from 1 to 512, 8320 in all
Outputs:
- leaving: bfloat16 [64, 128, 4096], P('section', None, 'head')
The draws below stay inside these ranges and needn't reach their ends.
Inputs may be any that keep to these rules, and one draw needn't show every extreme that they name: `entering`: entries of the activations that enter.
All inputs are finite; a program needn't handle non-finite values.
Results may differ from the reference program's by a relative error of at most 0.01.
Values may be sent and summed in bfloat16 or wider, within the bound.
A program may use at most 32 MiB of HBM per device.

```python
import math
import jax
import jax.numpy as jnp
import numpy as np
from jax import lax

HD = 128
HQ = 32
KVH = 4
SLICE = 128
GROUP = 8
DW = 4096
PACK = 8320
NDOC = 65
MOST = 512
N_SECTION = 64


def draw_entering(key, part):
    columns = jnp.arange(DW, dtype=jnp.float32) / DW
    raw_values = jax.random.truncated_normal(key, -6.0, 6.0, (N_SECTION, SLICE, DW), jnp.float32)
    return (raw_values * jnp.exp(columns * math.log(3.0))[None, None, :] / 3.0).astype(jnp.bfloat16)


def joint_weights(key):
    base_key = jax.random.fold_in(key, 101)
    kv_rows = jax.random.truncated_normal(jax.random.fold_in(base_key, 1), -4.0, 4.0, (N_SECTION, DW, 2 * KVH * HD), jnp.float32) / math.sqrt(DW)
    noise_part = jax.random.truncated_normal(jax.random.fold_in(base_key, 2), -4.0, 4.0, (N_SECTION, DW, HQ * HD), jnp.float32) / math.sqrt(DW)
    query_rows = noise_part
    return (query_rows, kv_rows)


def draw_w_query(key, part):
    return joint_weights(key)[0].astype(jnp.bfloat16)


def draw_w_key_value(key, part):
    return joint_weights(key)[1].astype(jnp.bfloat16)


def steps_of(rng, extent, shards, smallest, high):
    gain = 1.0
    for dim, shards_of in shards:
        heights = jax.random.uniform(jax.random.fold_in(jax.random.fold_in(rng, 6), dim), (shards_of,), jnp.float32, smallest / len(shards), high / len(shards))
        gain = gain * jnp.repeat(jnp.exp(heights), extent[dim] // shards_of).reshape((-1,) + (1,) * (len(extent) - 1 - dim))
    return gain


def profile(count, total, bound, slope):
    weights = [(1 << 20) // math.isqrt(rank ** slope) + 1 for rank in range(2, count + 1)]
    spare, holding = total - bound - (count - 1), [1] * (count - 1)
    while spare > 0:
        free = [i for i in range(count - 1) if holding[i] < bound]
        whole, left = sum([weights[i] for i in free]), spare
        for i in free:
            extra = min(bound - holding[i], max(1, left * weights[i] // whole), spare)
            holding[i] = holding[i] + extra
            spare = spare - extra
    return np.array([bound] + holding)


def ragged(key, amount, total, reach, slope):
    if amount == 2:
        one = jax.random.randint(key, (), max(1, total - reach), min(reach, total - 1) + 1)
        return jnp.stack([one, total - one])
    lengths = jnp.asarray(profile(amount, total, reach, slope), jnp.int32)
    couples = (amount - 1) // 2
    donor, receiver = lengths[1:1 + 2 * couples:2], lengths[2:2 + 2 * couples:2]
    slack = jnp.minimum(donor - 1, reach - receiver)
    shifted = jax.random.randint(jax.random.fold_in(key, 1), (couples,), 0, 1 << 20) % (slack + 1)
    lengths = lengths.at[1:1 + 2 * couples:2].set(donor - shifted).at[2:2 + 2 * couples:2].set(receiver + shifted)
    return lengths[jax.random.permutation(jax.random.fold_in(key, 2), amount)]


def scatter_about(key, dims, scale, bound, pieces=(), kind=jnp.bfloat16):
    drawn = scale * jax.random.normal(key, dims, jnp.float32)
    if pieces:
        drawn = drawn * steps_of(key, dims, pieces, -0.22, 0.18)
    return jnp.clip(drawn, -bound, bound).astype(kind)


def setup_inputs(seed: int = 0) -> dict:
    key_of = jax.random.split(jax.random.key(seed), 7)
    entering = draw_entering(jax.random.fold_in(key_of[6], 71), 0)
    fresh_slice = scatter_about(key_of[1], (SLICE, DW), 1.0, 6.0, ((1, 16),))
    norm_gain = jnp.clip(1.0 + 0.1 * jax.random.normal(key_of[2], (N_SECTION, DW), jnp.float32), 0.5, 1.5)
    w_query = draw_w_query(jax.random.fold_in(key_of[6], 71), 0)
    w_key_value = draw_w_key_value(jax.random.fold_in(key_of[6], 71), 0)
    doc_lengths = ragged(key_of[5], NDOC, PACK, MOST, 2).astype(jnp.int32)
    return {"entering": entering, "fresh_slice": fresh_slice, "norm_gain": norm_gain, "w_query": w_query, "w_key_value": w_key_value, "doc_lengths": doc_lengths}


epsilon = 1e-05
masked_score = -1e+30

def doc_index(position, doc_ends):
    return lax.optimization_barrier(jnp.sum((doc_ends[None, :] <= position[:, None]).astype(jnp.int32), axis=1))

def attend_block(query_block, query_pos, query_doc, all_keys, all_values, key_pos, key_doc):
    scores = jnp.einsum('qghd,kgd->ghqk', query_block.astype(jnp.float32), all_keys.astype(jnp.float32)) / math.sqrt(HD)
    allowed = (key_pos[None, :] <= query_pos[:, None]) & (key_doc[None, :] == query_doc[:, None])
    scores = jnp.where(allowed[None, None], scores, masked_score)
    row_max = lax.optimization_barrier(jnp.max(scores, axis=-1, keepdims=True))
    expon = jnp.exp(scores - row_max)
    weights = (expon / lax.optimization_barrier(jnp.sum(expon, axis=-1, keepdims=True))).astype(jnp.bfloat16)
    mixed = jnp.einsum('ghqk,kgd->qghd', weights.astype(jnp.float32), all_values.astype(jnp.float32))
    return mixed.astype(jnp.bfloat16)

def section_layer(row_data, gain_row, w_q, w_kv, start, doc_ends, resident):
    slice_len = row_data.shape[0]
    widened = row_data.astype(jnp.float32)
    mean_sq = lax.optimization_barrier(jnp.mean(widened * widened, axis=1, keepdims=True))
    normed = (widened * lax.rsqrt(mean_sq + epsilon) * gain_row[None, :]).astype(jnp.bfloat16)
    queries = jnp.dot(normed, w_q, preferred_element_type=jnp.float32).astype(jnp.bfloat16)
    packed = jnp.dot(normed, w_kv, preferred_element_type=jnp.float32).astype(jnp.bfloat16)
    packed = packed.reshape(slice_len, HD, KVH, 2)
    new_keys = jnp.transpose(packed[:, :, :, 0], (0, 2, 1))
    new_values = jnp.transpose(packed[:, :, :, 1], (0, 2, 1))
    position = start + jnp.arange(slice_len, dtype=jnp.int32)
    if resident is None:
        all_keys, all_values, key_pos = (new_keys, new_values, position)
    else:
        all_keys = jnp.concatenate([resident[0], new_keys], axis=0)
        all_values = jnp.concatenate([resident[1], new_values], axis=0)
        key_pos = jnp.concatenate([resident[2], position], axis=0)
    key_doc = doc_index(key_pos, doc_ends)
    query_doc = doc_index(position, doc_ends)
    block_len = min(512, slice_len)
    count = slice_len // block_len
    query_groups = queries.reshape(count, block_len, KVH, GROUP, HD)

    def one_block(block_args):
        return attend_block(block_args[0], block_args[1], block_args[2], all_keys, all_values, key_pos, key_doc)
    attended = lax.map(one_block, (query_groups, position.reshape(count, block_len), query_doc.reshape(count, block_len)))
    attended = attended.reshape(slice_len, HQ * HD).astype(jnp.float32)
    return ((widened + attended).astype(jnp.bfloat16), new_keys, new_values, position)

def reference(entering, fresh_slice, norm_gain, w_query, w_key_value, doc_lengths):
    doc_ends = jnp.cumsum(doc_lengths).astype(jnp.int32)
    sections = entering.shape[0]
    slice_len = entering.shape[1]
    section_ids = jnp.arange(sections, dtype=jnp.int32)

    def first_tick(packed_args):
        section_index, row_data, gain_row, w_q, w_kv = packed_args
        start = (sections - 1 - section_index) * slice_len
        return section_layer(row_data, gain_row, w_q, w_kv, start, doc_ends, None)
    first_out, keys_first, values_first, pos_first = lax.map(first_tick, (section_ids, entering, norm_gain, w_query, w_key_value))
    second_in = jnp.concatenate([fresh_slice[None], first_out[:-1]], axis=0)

    def second_tick(packed_args):
        section_index, row_data, gain_row, w_q, w_kv, old_keys, old_values, old_pos = packed_args
        start = (sections - section_index) * slice_len
        result = section_layer(row_data, gain_row, w_q, w_kv, start, doc_ends, (old_keys, old_values, old_pos))
        return result[0]
    return lax.map(second_tick, (section_ids, second_in, norm_gain, w_query, w_key_value, keys_first, values_first, pos_first))
```

```python
import functools
import math

import jax
import jax.numpy as jnp
from jax import lax
from jax.experimental import pallas as pl
from jax.experimental.pallas import tpu as pltpu
from jax.sharding import PartitionSpec as P

MESH = pl.DeviceIdType.MESH
HD = 128
KVH = 4
GROUP = 8
EPS = 1e-05
NEG = -1e30
PIECES = 4
F32 = jnp.float32
BF16 = jnp.bfloat16
NT = (((1,), (1,)), ((), ()))


def iota(shape, dim):
    return lax.broadcasted_iota(jnp.int32, shape, dim)


def body(
    x_hbm, fresh_hbm, gain_hbm, wq_hbm, wkv_hbm, len_hbm, out_hbm,
    xg, xn, wq, wkv, wkvp, gain, lens, lens_pad, fresh, obuf, kvst, kvbuf,
    acc, sq, bias1, bias2,
    load_sem, own_sem, out_sem, ring_recv, ring_send, mate_recv, mate_send,
    hop_recv, hop_send, kv_recv, kv_send, kv_own,
):
    sections = lax.axis_size("section")
    heads = lax.axis_size("head")
    chips = heads // 2
    tokens, width = obuf.shape
    rows = tokens // PIECES
    s = lax.axis_index("section")
    h = lax.axis_index("head")
    y, core = h // 2, h % 2
    mate = (s, y * 2 + (1 - core))
    following = (s + 1) % sections
    previous = (s + sections - 1) % sections

    def chip_at(offset):
        return (y + offset + chips) % chips

    def same_core(offset):
        return chip_at(offset) * 2 + core

    def other_core(offset):
        return chip_at(offset) * 2 + 1 - core

    right, left = same_core(1), same_core(-1)

    loads = [
        pltpu.make_async_copy(src, dst, load_sem.at[i])
        for i, (src, dst) in enumerate(
            ((gain_hbm, gain), (wkv_hbm, wkv), (len_hbm, lens), (fresh_hbm, fresh), (wq_hbm, wq))
        )
    ]
    own = pltpu.make_async_copy(x_hbm, xg.at[0, h], own_sem)
    own.start()
    for load in loads:
        load.start()

    barrier = pltpu.get_barrier_semaphore()
    greeted = [(s, (h + d) % heads) for d in range(1, heads)]
    for section in (following, previous):
        for other in (h, right, left):
            greeted.append((section, other))
    for device in greeted:
        pl.semaphore_signal(barrier, inc=1, device_id=device, device_id_type=MESH)
    pl.semaphore_wait(barrier, len(greeted))

    def piece(p):
        return pl.ds(p * rows, rows)

    def send(src, dst, send_sem, recv_sem, device):
        copy = pltpu.make_async_remote_copy(
            src_ref=src, dst_ref=dst, send_sem=send_sem, recv_sem=recv_sem,
            device_id=device, device_id_type=MESH,
        )
        copy.start()
        return copy

    def await_recv(ref, sem):
        pltpu.make_async_remote_copy(
            src_ref=ref, dst_ref=ref, send_sem=sem, recv_sem=sem,
            device_id=mate, device_id_type=MESH,
        ).wait_recv()

    def await_send(ref, sem):
        pltpu.make_async_remote_copy(
            src_ref=ref, dst_ref=ref, send_sem=sem, recv_sem=sem,
            device_id=mate, device_id_type=MESH,
        ).wait_send()

    dirs = ((0, -1, (s, right)), (1, 1, (s, left)))
    half = chips // 2
    halves = (range(0, PIECES // 2), range(PIECES // 2, PIECES))

    def forward(turn, step, p, d, target):
        chunk = xg.at[turn, same_core(step if d else -step), piece(p)]
        send(chunk, chunk, ring_send.at[turn], ring_recv.at[turn, d, step, p], target)

    def to_mate(turn, offset, sel, slot):
        chunk = xg.at[turn, same_core(offset), sel]
        send(chunk, chunk, mate_send.at[turn], mate_recv.at[turn, slot], mate)

    everything = pl.ds(0, tokens)

    def first_sends():
        for p in range(PIECES):
            for d, _, target in dirs:
                send(x_hbm.at[piece(p)], xg.at[0, h, piece(p)], ring_send.at[0],
                     ring_recv.at[0, d, 0, p], target)
        send(x_hbm, xg.at[0, h], mate_send.at[0], mate_recv.at[0, 0], mate)

    def prepare():
        for load in loads[:4]:
            load.wait()
        n = wkv.shape[0]
        r, c = iota((n, n), 0), iota((n, n), 1)
        perm = (((c % 8) // 2 == r // 16) & (c // 8 == r % 8) & (c % 2 == (r % 16) // 8))
        perm = perm.astype(F32).astype(BF16)
        for j in range(heads):
            wkvp[j] = jnp.dot(
                perm, wkv[:, j * width:(j + 1) * width], preferred_element_type=F32
            ).astype(BF16)
        docs = lens.shape[1]
        lens_pad[...] = jnp.zeros_like(lens_pad)
        lens_pad[:, 0:docs] = lens[...].astype(F32)
        n = lens_pad.shape[1]
        e0, e1 = iota((n, n), 0), iota((n, n), 1)
        row = jnp.broadcast_to(lens_pad[...], (n, n))
        far = F32(1e9)
        ends_col = jnp.sum(jnp.where(e1 <= e0, row, 0.0), axis=1, keepdims=True)
        ends_col = jnp.where(iota((n, 1), 0) < docs, ends_col, far)
        ends_row = jnp.sum(jnp.where(e0 == e1, ends_col, 0.0), axis=0, keepdims=True)
        start = ((sections - 1 - s) * tokens).astype(F32)
        def docs_of_rows(begin):
            pos = begin + iota((tokens, n), 0).astype(F32)
            return jnp.sum((ends_row <= pos).astype(F32), axis=1, keepdims=True)
        def docs_of_columns(begin):
            pos = begin + iota((n, tokens), 1).astype(F32)
            return jnp.sum((ends_col <= pos).astype(F32), axis=0, keepdims=True)
        q1, q2 = docs_of_rows(start), docs_of_rows(start + tokens)
        k1, k2 = docs_of_columns(start), docs_of_columns(start + tokens)
        causal = iota((tokens, tokens), 1) <= iota((tokens, tokens), 0)
        bias1[...] = jnp.where(causal & (q1 == k1), 0.0, NEG)
        bias2[:, 0:tokens] = jnp.where(q2 == k1, 0.0, NEG)
        bias2[:, tokens:2 * tokens] = jnp.where(causal & (q2 == k2), 0.0, NEG)

    def clear():
        acc[...] = jnp.zeros_like(acc)
        sq[...] = jnp.zeros_like(sq)

    def take(turn, j):
        wide = xg[turn, j].astype(F32)
        low, high = wide[:, 0:128], wide[:, 128:256]
        sq[...] += low * low + high * high
        at = pl.multiple_of(j * width, width)
        scaled = (wide * gain[:, pl.ds(at, width)]).astype(BF16)
        xn[:, pl.ds(at, width)] = scaled
        acc[...] += lax.dot_general(wkvp[j], scaled, NT, preferred_element_type=F32)

    def take_mate(turn, offset, slot):
        await_recv(xg.at[turn, 0], mate_recv.at[turn, slot])
        take(turn, other_core(offset))

    group = h * (width // HD) // GROUP
    sel_r, sel_c = iota((HD, 2 * HD), 0), iota((HD, 2 * HD), 1)
    same_peer = sel_r // 8 == sel_c // 16
    pick_key = (same_peer & (sel_c % 16 == sel_r % 8)).astype(F32).astype(BF16)
    pick_value = (same_peer & (sel_c % 16 == 8 + sel_r % 8)).astype(F32).astype(BF16)

    def exchange(turn):
        mean_sq = jnp.sum(sq[...], axis=1, keepdims=True) * (1.0 / (heads * width))
        scale = lax.rsqrt(mean_sq + EPS)
        diag = iota((tokens, tokens), 0) == iota((tokens, tokens), 1)
        scale_row = jnp.sum(jnp.where(diag, scale, 0.0), axis=0, keepdims=True)
        kvst[turn] = (acc[...] * scale_row).astype(BF16).reshape(KVH, 16, tokens)
        for d in range(1, heads):
            peer = (h + d) % heads
            send(kvst.at[turn, peer * (width // HD) // GROUP], kvbuf.at[turn, h],
                 kv_send.at[turn], kv_recv.at[turn], (s, peer))
        keep = pltpu.make_async_copy(kvst.at[turn, group], kvbuf.at[turn, h], kv_own.at[turn])
        keep.start()
        return scale, keep

    def queries(scale):
        q = jnp.dot(xn[...], wq[...], preferred_element_type=F32)
        q = (q * scale).astype(BF16)
        spread = [
            jnp.dot(q[:, i * HD:(i + 1) * HD], pick_key, preferred_element_type=F32)
            for i in range(width // HD)
        ]
        return jnp.concatenate(spread, axis=0).astype(BF16)

    def await_kv(turn, keep):
        keep.wait()
        await_recv(kvbuf.at[turn, pl.ds(0, heads - 1)], kv_recv.at[turn])

    def attend(turn, wide_q, bias):
        here = width // HD
        turns = range(turn + 1)
        both = [kvbuf[t].reshape(heads * 16, tokens) for t in turns]
        scores = [
            jnp.dot(wide_q, kv, preferred_element_type=F32) * (1.0 / math.sqrt(HD)) for kv in both
        ]
        scores = jnp.concatenate(scores, axis=1) + jnp.concatenate([bias[...]] * here, axis=0)
        expon = jnp.exp(scores - jnp.max(scores, axis=1, keepdims=True))
        weights = (expon / jnp.sum(expon, axis=1, keepdims=True)).astype(BF16)
        values = [
            jnp.dot(pick_value, kv, preferred_element_type=F32).astype(BF16) for kv in both
        ]
        values = jnp.concatenate(values, axis=1)
        mixed = lax.dot_general(weights, values, NT, preferred_element_type=F32).astype(BF16)
        for i in range(here):
            cols = slice(i * HD, (i + 1) * HD)
            total = xg[turn, h, :, cols].astype(F32) + mixed[i * tokens:(i + 1) * tokens].astype(F32)
            if turn == 0:
                total = jnp.where(s == sections - 1, fresh[:, cols].astype(F32), total)
            obuf[:, cols] = total.astype(BF16)

    def rest_of_ring(turn, step):
        for p in range(PIECES):
            for d, sign, target in dirs:
                if step == half and p not in halves[d]:
                    continue
                chunk = xg.at[turn, same_core(sign * step), piece(p)]
                await_recv(chunk, ring_recv.at[turn, d, step - 1, p])
                if step < half - 1 or (step == half - 1 and p in halves[d]):
                    forward(turn, step, p, d, target)
                slot = 2 * step - 1 + (d if step < half else 0)
                to_mate(turn, sign * step, piece(p), slot)

    def take_step(turn, step):
        take(turn, same_core(-step))
        if step < half:
            take(turn, same_core(step))
        take_mate(turn, -step, 2 * step - 1)
        if step < half:
            take_mate(turn, step, 2 * step)

    first_sends()
    clear()
    prepare()
    own.wait()
    take(0, h)
    take_mate(0, 0, 0)
    for step in range(1, half + 1):
        rest_of_ring(0, step)
        if step > 1:
            take_step(0, step - 1)
    take_step(0, half)
    scale, keep = exchange(0)
    loads[4].wait()
    wide_q = queries(scale)
    await_kv(0, keep)
    attend(0, wide_q, bias1)

    for p in range(PIECES):
        for slot, other in ((0, h), (1, right), (2, left)):
            send(obuf.at[piece(p)], xg.at[1, h, piece(p)], hop_send,
                 hop_recv.at[p] if slot == 0 else ring_recv.at[1, slot - 1, 0, p],
                 (following, other))

    clear()
    for p in range(PIECES):
        await_recv(xg.at[1, h, piece(p)], hop_recv.at[p])
        to_mate(1, 0, piece(p), 0)
    for step in range(1, half + 1):
        rest_of_ring(1, step)
        if step == 1:
            take(1, h)
            take_mate(1, 0, 0)
        else:
            take_step(1, step - 1)
    take_step(1, half)
    scale, keep = exchange(1)
    wide_q = queries(scale)
    await_kv(1, keep)
    for _ in range(3):
        pass
    await_send(xg.at[0, pl.ds(0, 3)], hop_send)
    attend(1, wide_q, bias2)
    result = pltpu.make_async_copy(obuf, out_hbm, out_sem)
    result.start()

    await_send(xg.at[0, pl.ds(0, 2 * half - 1)], ring_send.at[0])
    await_send(xg.at[1, pl.ds(0, 2 * half - 3)], ring_send.at[1])
    for turn in range(2):
        await_send(xg.at[turn, pl.ds(0, 2 * half)], mate_send.at[turn])
        await_send(kvbuf.at[turn, pl.ds(0, heads - 1)], kv_send.at[turn])
    result.wait()


def solution(mesh):
    heads = mesh.shape["head"]
    half = heads // 4

    def shards(entering, fresh_slice, norm_gain, w_query, w_key_value, doc_lengths):
        _, tokens, width = entering.shape
        features = w_query.shape[1]
        columns = w_key_value.shape[2]
        docs = doc_lengths.shape[0]
        any_spec = pl.BlockSpec(memory_space=pl.ANY)
        dma = pltpu.SemaphoreType.DMA
        out = pl.pallas_call(
            body,
            out_shape=jax.ShapeDtypeStruct((tokens, width), BF16),
            in_specs=[any_spec] * 6,
            out_specs=any_spec,
            scratch_shapes=[
                pltpu.VMEM((2, heads, tokens, width), BF16),
                pltpu.VMEM((tokens, features), BF16),
                pltpu.VMEM((features, width), BF16),
                pltpu.VMEM((columns, features), BF16),
                pltpu.VMEM((heads, columns, width), BF16),
                pltpu.VMEM((1, features), F32),
                pltpu.VMEM((1, docs), jnp.int32),
                pltpu.VMEM((1, 128), F32),
                pltpu.VMEM((tokens, width), BF16),
                pltpu.VMEM((tokens, width), BF16),
                pltpu.VMEM((2, KVH, 16, tokens), BF16),
                pltpu.VMEM((2, heads, 16, tokens), BF16),
                pltpu.VMEM((columns, tokens), F32),
                pltpu.VMEM((tokens, 128), F32),
                pltpu.VMEM((tokens, tokens), F32),
                pltpu.VMEM((tokens, 2 * tokens), F32),
                dma((5,)),
                dma,
                dma,
                dma((2, 2, half, PIECES)),
                dma((2,)),
                dma((2, 2 * half)),
                dma((2,)),
                dma((PIECES,)),
                dma,
                dma((2,)),
                dma((2,)),
                dma((2,)),
            ],
            compiler_params=pltpu.CompilerParams(collective_id=0, has_side_effects=True),
        )(
            entering[0], fresh_slice, norm_gain, w_query[0], w_key_value[0].T,
            doc_lengths.reshape(1, docs),
        )
        return out[None]

    placed = (
        P("section", None, "head"),
        P(None, "head"),
        P("section", None),
        P("section", None, "head"),
        P("section", None, "head"),
        P(),
    )
    return jax.shard_map(
        shards, mesh=mesh, in_specs=placed, out_specs=P("section", None, "head"), check_vma=False
    )
```

```python
import functools
import math

import jax
import jax.numpy as jnp
from jax import lax
from jax.experimental import pallas as pl
from jax.experimental.pallas import tpu as pltpu
from jax.sharding import PartitionSpec as P

MESH = pl.DeviceIdType.MESH
HD = 128
KVH = 4
GROUP = 8
EPS = 1e-05
NEG = -1e30
PIECES = 4
F32 = jnp.float32
BF16 = jnp.bfloat16
NT = (((1,), (1,)), ((), ()))


def iota(shape, dim):
    return lax.broadcasted_iota(jnp.int32, shape, dim)


def body(
    x_hbm, fresh_hbm, gain_hbm, wq_hbm, wkv_hbm, len_hbm, out_hbm,
    xg, xn, wq, wkv, wkvp, gain, lens, lens_pad, fresh, obuf, kvst, kvbuf,
    acc, sq, bias1, bias2,
    load_sem, own_sem, out_sem, ring_recv, ring_send, mate_recv, mate_send,
    hop_recv, hop_send, kv_recv, kv_send, kv_own,
):
    sections = lax.axis_size("section")
    heads = lax.axis_size("head")
    chips = heads // 2
    tokens, width = obuf.shape
    rows = tokens // PIECES
    s = lax.axis_index("section")
    h = lax.axis_index("head")
    y, core = h // 2, h % 2
    mate = (s, y * 2 + (1 - core))
    following = (s + 1) % sections
    previous = (s + sections - 1) % sections

    def chip_at(offset):
        return (y + offset + chips) % chips

    def same_core(offset):
        return chip_at(offset) * 2 + core

    def other_core(offset):
        return chip_at(offset) * 2 + 1 - core

    right, left = same_core(1), same_core(-1)

    loads = [
        pltpu.make_async_copy(src, dst, load_sem.at[i])
        for i, (src, dst) in enumerate(
            ((gain_hbm, gain), (wkv_hbm, wkv), (len_hbm, lens), (fresh_hbm, fresh), (wq_hbm, wq))
        )
    ]
    own = pltpu.make_async_copy(x_hbm, xg.at[0, h], own_sem)
    own.start()
    for load in loads:
        load.start()

    barrier = pltpu.get_barrier_semaphore()
    near = (h, right, left)
    for device in [mate, (s, right), (s, left)] + [(previous, other) for other in near]:
        pl.semaphore_signal(barrier, inc=1, device_id=device, device_id_type=MESH)
    pl.semaphore_wait(barrier, 6)

    def piece(p):
        return pl.ds(p * rows, rows)

    def send(src, dst, send_sem, recv_sem, device):
        copy = pltpu.make_async_remote_copy(
            src_ref=src, dst_ref=dst, send_sem=send_sem, recv_sem=recv_sem,
            device_id=device, device_id_type=MESH,
        )
        copy.start()
        return copy

    def await_recv(ref, sem):
        pltpu.make_async_remote_copy(
            src_ref=ref, dst_ref=ref, send_sem=sem, recv_sem=sem,
            device_id=mate, device_id_type=MESH,
        ).wait_recv()

    def await_send(ref, sem):
        pltpu.make_async_remote_copy(
            src_ref=ref, dst_ref=ref, send_sem=sem, recv_sem=sem,
            device_id=mate, device_id_type=MESH,
        ).wait_send()

    dirs = ((0, -1, (s, right)), (1, 1, (s, left)))
    half = chips // 2
    halves = (range(0, PIECES // 2), range(PIECES // 2, PIECES))

    def forward(turn, step, p, d, target):
        chunk = xg.at[turn, same_core(step if d else -step), piece(p)]
        send(chunk, chunk, ring_send.at[turn], ring_recv.at[turn, d, step, p], target)

    def to_mate(turn, offset, sel, slot):
        chunk = xg.at[turn, same_core(offset), sel]
        send(chunk, chunk, mate_send.at[turn], mate_recv.at[turn, slot], mate)

    everything = pl.ds(0, tokens)

    def first_sends():
        for p in range(PIECES):
            for d, _, target in dirs:
                send(x_hbm.at[piece(p)], xg.at[0, h, piece(p)], ring_send.at[0],
                     ring_recv.at[0, d, 0, p], target)
        send(x_hbm, xg.at[0, h], mate_send.at[0], mate_recv.at[0, 0], mate)

    def prepare():
        for load in loads[:4]:
            load.wait()
        n = wkv.shape[0]
        r, c = iota((n, n), 0), iota((n, n), 1)
        perm = (((c % 8) // 2 == r // 16) & (c // 8 == r % 8) & (c % 2 == (r % 16) // 8))
        perm = perm.astype(F32).astype(BF16)
        for j in range(heads):
            wkvp[j] = jnp.dot(
                perm, wkv[:, j * width:(j + 1) * width], preferred_element_type=F32
            ).astype(BF16)
        docs = lens.shape[1]
        lens_pad[...] = jnp.zeros_like(lens_pad)
        lens_pad[:, 0:docs] = lens[...].astype(F32)
        n = lens_pad.shape[1]
        e0, e1 = iota((n, n), 0), iota((n, n), 1)
        row = jnp.broadcast_to(lens_pad[...], (n, n))
        far = F32(1e9)
        ends_col = jnp.sum(jnp.where(e1 <= e0, row, 0.0), axis=1, keepdims=True)
        ends_col = jnp.where(iota((n, 1), 0) < docs, ends_col, far)
        ends_row = jnp.sum(jnp.where(e0 == e1, ends_col, 0.0), axis=0, keepdims=True)
        start = ((sections - 1 - s) * tokens).astype(F32)
        def docs_of_rows(begin):
            pos = begin + iota((tokens, n), 0).astype(F32)
            return jnp.sum((ends_row <= pos).astype(F32), axis=1, keepdims=True)
        def docs_of_columns(begin):
            pos = begin + iota((n, tokens), 1).astype(F32)
            return jnp.sum((ends_col <= pos).astype(F32), axis=0, keepdims=True)
        q1, q2 = docs_of_rows(start), docs_of_rows(start + tokens)
        k1, k2 = docs_of_columns(start), docs_of_columns(start + tokens)
        causal = iota((tokens, tokens), 1) <= iota((tokens, tokens), 0)
        bias1[...] = jnp.where(causal & (q1 == k1), 0.0, NEG)
        bias2[:, 0:tokens] = jnp.where(q2 == k1, 0.0, NEG)
        bias2[:, tokens:2 * tokens] = jnp.where(causal & (q2 == k2), 0.0, NEG)

    def clear():
        acc[...] = jnp.zeros_like(acc)
        sq[...] = jnp.zeros_like(sq)

    def take(turn, j):
        wide = xg[turn, j].astype(F32)
        low, high = wide[:, 0:128], wide[:, 128:256]
        sq[...] += low * low + high * high
        at = pl.multiple_of(j * width, width)
        scaled = (wide * gain[:, pl.ds(at, width)]).astype(BF16)
        xn[:, pl.ds(at, width)] = scaled
        acc[...] += lax.dot_general(wkvp[j], scaled, NT, preferred_element_type=F32)

    def take_mate(turn, offset, slot):
        await_recv(xg.at[turn, 0], mate_recv.at[turn, slot])
        take(turn, other_core(offset))

    group = h * (width // HD) // GROUP
    sel_r, sel_c = iota((HD, 2 * HD), 0), iota((HD, 2 * HD), 1)
    same_peer = sel_r // 8 == sel_c // 16
    pick_key = (same_peer & (sel_c % 16 == sel_r % 8)).astype(F32).astype(BF16)
    pick_value = (same_peer & (sel_c % 16 == 8 + sel_r % 8)).astype(F32).astype(BF16)

    def exchange(turn):
        mean_sq = jnp.sum(sq[...], axis=1, keepdims=True) * (1.0 / (heads * width))
        scale = lax.rsqrt(mean_sq + EPS)
        diag = iota((tokens, tokens), 0) == iota((tokens, tokens), 1)
        scale_row = jnp.sum(jnp.where(diag, scale, 0.0), axis=0, keepdims=True)
        kvst[turn] = (acc[...] * scale_row).astype(BF16).reshape(KVH, 16, tokens)
        for d in range(1, heads):
            peer = (h + d) % heads
            send(kvst.at[turn, peer * (width // HD) // GROUP], kvbuf.at[turn, h],
                 kv_send.at[turn], kv_recv.at[turn], (s, peer))
        keep = pltpu.make_async_copy(kvst.at[turn, group], kvbuf.at[turn, h], kv_own.at[turn])
        keep.start()
        return scale, keep

    def queries(scale):
        q = jnp.dot(xn[...], wq[...], preferred_element_type=F32)
        q = (q * scale).astype(BF16)
        spread = [
            jnp.dot(q[:, i * HD:(i + 1) * HD], pick_key, preferred_element_type=F32)
            for i in range(width // HD)
        ]
        return jnp.concatenate(spread, axis=0).astype(BF16)

    def await_kv(turn, keep):
        keep.wait()
        await_recv(kvbuf.at[turn, pl.ds(0, heads - 1)], kv_recv.at[turn])

    def attend(turn, wide_q, bias):
        here = width // HD
        turns = range(turn + 1)
        both = [kvbuf[t].reshape(heads * 16, tokens) for t in turns]
        scores = [
            jnp.dot(wide_q, kv, preferred_element_type=F32) * (1.0 / math.sqrt(HD)) for kv in both
        ]
        scores = jnp.concatenate(scores, axis=1) + jnp.concatenate([bias[...]] * here, axis=0)
        expon = jnp.exp(scores - jnp.max(scores, axis=1, keepdims=True))
        weights = (expon / jnp.sum(expon, axis=1, keepdims=True)).astype(BF16)
        values = [
            jnp.dot(pick_value, kv, preferred_element_type=F32).astype(BF16) for kv in both
        ]
        values = jnp.concatenate(values, axis=1)
        mixed = lax.dot_general(weights, values, NT, preferred_element_type=F32).astype(BF16)
        for i in range(here):
            cols = slice(i * HD, (i + 1) * HD)
            total = xg[turn, h, :, cols].astype(F32) + mixed[i * tokens:(i + 1) * tokens].astype(F32)
            if turn == 0:
                total = jnp.where(s == sections - 1, fresh[:, cols].astype(F32), total)
            obuf[:, cols] = total.astype(BF16)

    def rest_of_ring(turn, step):
        for p in range(PIECES):
            for d, sign, target in dirs:
                if step == half and p not in halves[d]:
                    continue
                chunk = xg.at[turn, same_core(sign * step), piece(p)]
                await_recv(chunk, ring_recv.at[turn, d, step - 1, p])
                if step < half - 1 or (step == half - 1 and p in halves[d]):
                    forward(turn, step, p, d, target)
                slot = 2 * step - 1 + (d if step < half else 0)
                to_mate(turn, sign * step, piece(p), slot)

    def take_step(turn, step):
        take(turn, same_core(-step))
        if step < half:
            take(turn, same_core(step))
        take_mate(turn, -step, 2 * step - 1)
        if step < half:
            take_mate(turn, step, 2 * step)

    first_sends()
    clear()
    prepare()
    own.wait()
    take(0, h)
    take_mate(0, 0, 0)
    for step in range(1, half + 1):
        rest_of_ring(0, step)
        if step > 1:
            take_step(0, step - 1)
    take_step(0, half)
    scale, keep = exchange(0)
    loads[4].wait()
    wide_q = queries(scale)
    await_kv(0, keep)
    attend(0, wide_q, bias1)

    for p in range(PIECES):
        for slot, other in ((0, h), (1, right), (2, left)):
            send(obuf.at[piece(p)], xg.at[1, h, piece(p)], hop_send,
                 hop_recv.at[p] if slot == 0 else ring_recv.at[1, slot - 1, 0, p],
                 (following, other))

    clear()
    for p in range(PIECES):
        await_recv(xg.at[1, h, piece(p)], hop_recv.at[p])
        to_mate(1, 0, piece(p), 0)
    for step in range(1, half + 1):
        rest_of_ring(1, step)
        if step == 1:
            take(1, h)
            take_mate(1, 0, 0)
        else:
            take_step(1, step - 1)
    take_step(1, half)
    scale, keep = exchange(1)
    wide_q = queries(scale)
    await_kv(1, keep)
    await_send(xg.at[0, pl.ds(0, 3)], hop_send)
    attend(1, wide_q, bias2)
    result = pltpu.make_async_copy(obuf, out_hbm, out_sem)
    result.start()

    await_send(xg.at[0, pl.ds(0, 2 * half - 1)], ring_send.at[0])
    await_send(xg.at[1, pl.ds(0, 2 * half - 3)], ring_send.at[1])
    for turn in range(2):
        await_send(xg.at[turn, pl.ds(0, 2 * half)], mate_send.at[turn])
        await_send(kvbuf.at[turn, pl.ds(0, heads - 1)], kv_send.at[turn])
    result.wait()


def solution(mesh):
    heads = mesh.shape["head"]
    half = heads // 4

    def shards(entering, fresh_slice, norm_gain, w_query, w_key_value, doc_lengths):
        _, tokens, width = entering.shape
        features = w_query.shape[1]
        columns = w_key_value.shape[2]
        docs = doc_lengths.shape[0]
        any_spec = pl.BlockSpec(memory_space=pl.ANY)
        dma = pltpu.SemaphoreType.DMA
        out = pl.pallas_call(
            body,
            out_shape=jax.ShapeDtypeStruct((tokens, width), BF16),
            in_specs=[any_spec] * 6,
            out_specs=any_spec,
            scratch_shapes=[
                pltpu.VMEM((2, heads, tokens, width), BF16),
                pltpu.VMEM((tokens, features), BF16),
                pltpu.VMEM((features, width), BF16),
                pltpu.VMEM((columns, features), BF16),
                pltpu.VMEM((heads, columns, width), BF16),
                pltpu.VMEM((1, features), F32),
                pltpu.VMEM((1, docs), jnp.int32),
                pltpu.VMEM((1, 128), F32),
                pltpu.VMEM((tokens, width), BF16),
                pltpu.VMEM((tokens, width), BF16),
                pltpu.VMEM((2, KVH, 16, tokens), BF16),
                pltpu.VMEM((2, heads, 16, tokens), BF16),
                pltpu.VMEM((columns, tokens), F32),
                pltpu.VMEM((tokens, 128), F32),
                pltpu.VMEM((tokens, tokens), F32),
                pltpu.VMEM((tokens, 2 * tokens), F32),
                dma((5,)),
                dma,
                dma,
                dma((2, 2, half, PIECES)),
                dma((2,)),
                dma((2, 2 * half)),
                dma((2,)),
                dma((PIECES,)),
                dma,
                dma((2,)),
                dma((2,)),
                dma((2,)),
            ],
            compiler_params=pltpu.CompilerParams(collective_id=0, has_side_effects=True),
        )(
            entering[0], fresh_slice, norm_gain, w_query[0], w_key_value[0].T,
            doc_lengths.reshape(1, docs),
        )
        return out[None]

    placed = (
        P("section", None, "head"),
        P(None, "head"),
        P("section", None),
        P("section", None, "head"),
        P("section", None, "head"),
        P(),
    )
    return jax.shard_map(
        shards, mesh=mesh, in_specs=placed, out_specs=P("section", None, "head"), check_vma=False
    )
```

```python
import functools
import math

import jax
import jax.numpy as jnp
from jax import lax
from jax.experimental import pallas as pl
from jax.experimental.pallas import tpu as pltpu
from jax.sharding import PartitionSpec as P

MESH = pl.DeviceIdType.MESH
HD = 128
KVH = 4
GROUP = 8
EPS = 1e-05
NEG = -1e30
PIECES = 4
F32 = jnp.float32
BF16 = jnp.bfloat16
NT = (((1,), (1,)), ((), ()))


def iota(shape, dim):
    return lax.broadcasted_iota(jnp.int32, shape, dim)


def body(
    x_hbm, fresh_hbm, gain_hbm, wq_hbm, wkv_hbm, len_hbm, out_ref,
    xg, xn, wq, wkv_raw, wkv, gain, lens, lens_pad, fresh, first, kvst, kvbuf,
    acc, sq, part_out, part_in, query_out, query_in, bias1, bias2,
    load_sem, own_sem, swap_send, swap_recv, ring_recv, ring_send, hop_send,
    part_send, part_recv, query_send, query_recv, kv_recv, kv_send, kv_own,
):
    sections = lax.axis_size("section")
    heads = lax.axis_size("head")
    chips = heads // 2
    tokens, width = first.shape
    columns = wkv_hbm.shape[0]
    rows = tokens // PIECES
    here = width // HD
    s = lax.axis_index("section")
    h = lax.axis_index("head")
    y, core = h // 2, h % 2
    mate = (s, y * 2 + (1 - core))
    following = ((s + 1) % sections, h)
    previous = ((s + sections - 1) % sections, h)

    def chip(offset):
        return (y + offset + chips) % chips

    def peer(offset):
        return (s, chip(offset) * 2 + core)

    def send(src, dst, send_sem, recv_sem, device):
        pltpu.make_async_remote_copy(
            src_ref=src, dst_ref=dst, send_sem=send_sem, recv_sem=recv_sem,
            device_id=device, device_id_type=MESH,
        ).start()

    def await_recv(ref, sem):
        pltpu.make_async_remote_copy(
            src_ref=ref, dst_ref=ref, send_sem=sem, recv_sem=sem,
            device_id=mate, device_id_type=MESH,
        ).wait_recv()

    def await_send(ref, sem):
        pltpu.make_async_remote_copy(
            src_ref=ref, dst_ref=ref, send_sem=sem, recv_sem=sem,
            device_id=mate, device_id_type=MESH,
        ).wait_send()

    def piece(p):
        return pl.ds(p * rows, rows)

    barrier = pltpu.get_barrier_semaphore()
    greeted = [mate, peer(1), peer(-1), peer(2), peer(-2), previous]
    for device in greeted:
        pl.semaphore_signal(barrier, inc=1, device_id=device, device_id_type=MESH)

    own = pltpu.make_async_copy(x_hbm, xg.at[0, y], own_sem)
    own.start()
    loads = [
        pltpu.make_async_copy(src, dst, load_sem.at[i])
        for i, (src, dst) in enumerate(
            ((gain_hbm, gain), (len_hbm, lens), (fresh_hbm, fresh), (wq_hbm.at[:, core], wq.at[0]))
        )
    ]
    for load in loads:
        load.start()

    def lanes(k, parity):
        return pl.ds(pl.multiple_of((2 * k + parity) * width, width), width)

    for k in range(chips):
        pltpu.make_async_copy(
            wkv_hbm.at[:, lanes(k, core)], wkv_raw.at[0, k], load_sem.at[4]
        ).start()
    pl.semaphore_wait(barrier, len(greeted))

    half = chips // 2
    halves = (range(0, PIECES // 2), range(PIECES // 2, PIECES))
    sides = ((0, 1), (1, -1))
    passed_by = {1: 0, 2: 0, 3: 2, 4: 2}

    def pieces(k, d):
        return range(PIECES) if k < half else halves[d]

    def pass_on(turn, k, p, d, src=None):
        sign = sides[d][1]
        owner = chip(-sign * k)
        chunk = xg.at[turn, owner, piece(p)]
        for k2 in (4, 3, 2, 1):
            if passed_by[k2] == k and k2 > k and p in pieces(k2, d):
                send(chunk if src is None else src, chunk, ring_send.at[turn],
                     ring_recv.at[turn, d, k2, p], peer(sign * (k2 - k)))

    def await_ring(turn, k):
        for p in range(PIECES):
            for d, sign in sides:
                if p in pieces(k, d):
                    await_recv(xg.at[turn, chip(-sign * k), piece(p)], ring_recv.at[turn, d, k, p])
                    pass_on(turn, k, p, d)

    def swap_weights():
        for k in range(chips):
            send(wkv_hbm.at[:, lanes(k, 1 - core)], wkv_raw.at[1, k], swap_send.at[0],
                 swap_recv.at[0], mate)
        send(wq_hbm.at[:, 1 - core], wq.at[1], swap_send.at[1], swap_recv.at[1], mate)

    def prepare():
        for load in loads[:3]:
            load.wait()
        docs = lens.shape[1]
        lens_pad[...] = jnp.zeros_like(lens_pad)
        lens_pad[:, 0:docs] = lens[...].astype(F32)
        n = lens_pad.shape[1]
        e0, e1 = iota((n, n), 0), iota((n, n), 1)
        row = jnp.broadcast_to(lens_pad[...], (n, n))
        far = F32(1e9)
        ends_col = jnp.sum(jnp.where(e1 <= e0, row, 0.0), axis=1, keepdims=True)
        ends_col = jnp.where(iota((n, 1), 0) < docs, ends_col, far)
        ends_row = jnp.sum(jnp.where(e0 == e1, ends_col, 0.0), axis=0, keepdims=True)
        start = ((sections - 1 - s) * tokens).astype(F32)

        def docs_of_rows(begin):
            pos = begin + iota((tokens, n), 0).astype(F32)
            return jnp.sum((ends_row <= pos).astype(F32), axis=1, keepdims=True)

        def docs_of_columns(begin):
            pos = begin + iota((n, tokens), 1).astype(F32)
            return jnp.sum((ends_col <= pos).astype(F32), axis=0, keepdims=True)

        q1, q2 = docs_of_rows(start), docs_of_rows(start + tokens)
        k1, k2 = docs_of_columns(start), docs_of_columns(start + tokens)
        causal = iota((tokens, tokens), 1) <= iota((tokens, tokens), 0)
        bias1[...] = jnp.where(causal & (q1 == k1), 0.0, NEG)
        bias2[:, 0:tokens] = jnp.where(q2 == k1, 0.0, NEG)
        bias2[:, tokens:2 * tokens] = jnp.where(causal & (q2 == k2), 0.0, NEG)
        r, c = iota((columns, columns), 0), iota((columns, columns), 1)
        perm = (((c % 8) // 2 == r // 16) & (c // 8 == r % 8) & (c % 2 == (r % 16) // 8))
        perm = perm.astype(F32).astype(BF16)
        pltpu.make_async_copy(wkv_raw.at[0], wkv_raw.at[0], load_sem.at[4]).wait()
        await_recv(wkv_raw.at[1], swap_recv.at[0])
        for k in range(chips):
            for side in range(2):
                wkv[k, side * columns:(side + 1) * columns] = jnp.dot(
                    perm, wkv_raw[side, k], preferred_element_type=F32
                ).astype(BF16)

    def clear():
        acc[...] = jnp.zeros_like(acc)
        sq[...] = jnp.zeros_like(sq)

    def take(turn, offset):
        k = chip(offset)
        wide = xg[turn, k].astype(F32)
        low, high = wide[:, 0:128], wide[:, 128:256]
        sq[...] += low * low + high * high
        scaled = (wide * gain[:, lanes(k, core)]).astype(BF16)
        xn[:, pl.ds(pl.multiple_of(k * width, width), width)] = scaled
        acc[...] += lax.dot_general(wkv[k], scaled, NT, preferred_element_type=F32)

    def take_both(turn, k):
        take(turn, -k)
        if k < half:
            take(turn, k)

    group = h * here // GROUP
    sel_r, sel_c = iota((HD, 2 * HD), 0), iota((HD, 2 * HD), 1)
    same_peer = sel_r // 8 == sel_c // 16
    pick_key = (same_peer & (sel_c % 16 == sel_r % 8)).astype(F32).astype(BF16)
    pick_value = (same_peer & (sel_c % 16 == 8 + sel_r % 8)).astype(F32).astype(BF16)
    diag = iota((tokens, tokens), 0) == iota((tokens, tokens), 1)

    def exchange(turn):
        square = jnp.sum(sq[...], axis=1, keepdims=True)
        square = jnp.sum(jnp.where(diag, square, 0.0), axis=0, keepdims=True)
        part_out[turn, 0:columns] = acc[columns:2 * columns]
        part_out[turn, columns:columns + 8] = jnp.broadcast_to(square, (8, tokens))
        send(part_out.at[turn], part_in.at[turn], part_send.at[turn], part_recv.at[turn], mate)
        await_recv(part_in.at[turn], part_recv.at[turn])
        square = square + part_in[turn, columns:columns + 1]
        scale = lax.rsqrt(square * (1.0 / (heads * width)) + EPS)
        total = acc[0:columns] + part_in[turn, 0:columns]
        kvst[turn] = (total * scale).astype(BF16).reshape(KVH, 16, tokens)
        for d in range(1, heads):
            other = (h + d) % heads
            send(kvst.at[turn, other * here // GROUP], kvbuf.at[turn, h],
                 kv_send.at[turn], kv_recv.at[turn], (s, other))
        keep = pltpu.make_async_copy(kvst.at[turn, group], kvbuf.at[turn, h], kv_own.at[turn])
        keep.start()
        return scale, keep

    def queries(turn, scale):
        def product(side):
            w = wq[side].reshape(chips * width, width)
            return jnp.dot(xn[...], w, preferred_element_type=F32)

        query_out[turn] = product(1)
        send(query_out.at[turn], query_in.at[turn], query_send.at[turn], query_recv.at[turn], mate)
        q = product(0)
        scale = jnp.sum(jnp.where(diag, scale, 0.0), axis=1, keepdims=True)
        await_recv(query_in.at[turn], query_recv.at[turn])
        q = ((q + query_in[turn]) * scale).astype(BF16)
        spread = [
            jnp.dot(q[:, i * HD:(i + 1) * HD], pick_key, preferred_element_type=F32)
            for i in range(here)
        ]
        return jnp.concatenate(spread, axis=0).astype(BF16)

    def await_kv(turn, keep):
        keep.wait()
        await_recv(kvbuf.at[turn, pl.ds(0, heads - 1)], kv_recv.at[turn])

    def attend(turn, wide_q, bias):
        both = [kvbuf[t].reshape(heads * 16, tokens) for t in range(turn + 1)]
        scores = [
            jnp.dot(wide_q, kv, preferred_element_type=F32) * (1.0 / math.sqrt(HD)) for kv in both
        ]
        scores = jnp.concatenate(scores, axis=1) + jnp.concatenate([bias[...]] * here, axis=0)
        expon = jnp.exp(scores - jnp.max(scores, axis=1, keepdims=True))
        weights = (expon / jnp.sum(expon, axis=1, keepdims=True)).astype(BF16)
        values = [
            jnp.dot(pick_value, kv, preferred_element_type=F32).astype(BF16) for kv in both
        ]
        values = jnp.concatenate(values, axis=1)
        mixed = lax.dot_general(weights, values, NT, preferred_element_type=F32).astype(BF16)
        mixed = mixed.astype(F32)
        for i in range(here):
            cols = slice(i * HD, (i + 1) * HD)
            total = xg[turn, y, :, cols].astype(F32) + mixed[i * tokens:(i + 1) * tokens]
            if turn == 0:
                total = jnp.where(s == sections - 1, fresh[:, cols].astype(F32), total)
                first[:, cols] = total.astype(BF16)
            else:
                out_ref[:, cols] = total.astype(BF16)

    def rest_of_gather(turn):
        await_ring(turn, 2)
        take(turn, 0)
        await_ring(turn, 1)
        take_both(turn, 1)
        take_both(turn, 2)
        await_ring(turn, 3)
        take_both(turn, 3)
        await_ring(turn, 4)
        take_both(turn, 4)

    for p in range(PIECES):
        for d, _ in sides:
            pass_on(0, 0, p, d, x_hbm.at[piece(p)])
    swap_weights()
    clear()
    prepare()
    own.wait()
    rest_of_gather(0)
    scale, keep = exchange(0)
    loads[3].wait()
    await_recv(wq.at[1], swap_recv.at[1])
    wide_q = queries(0, scale)
    await_kv(0, keep)
    attend(0, wide_q, bias1)

    for p in range(PIECES):
        send(first.at[piece(p)], xg.at[1, y, piece(p)], hop_send, ring_recv.at[1, 0, 0, p], following)

    clear()
    for p in range(PIECES):
        await_recv(xg.at[1, y, piece(p)], ring_recv.at[1, 0, 0, p])
        for d, _ in sides:
            pass_on(1, 0, p, d)
    rest_of_gather(1)
    scale, keep = exchange(1)
    wide_q = queries(1, scale)
    await_kv(1, keep)
    attend(1, wide_q, bias2)

    await_send(first, hop_send)
    await_send(wkv_raw.at[1], swap_send.at[0])
    await_send(wq.at[1], swap_send.at[1])
    for turn in range(2):
        await_send(xg.at[turn, pl.ds(0, 2 * half - 1)], ring_send.at[turn])
        await_send(part_out.at[turn], part_send.at[turn])
        await_send(query_out.at[turn], query_send.at[turn])
        await_send(kvbuf.at[turn, pl.ds(0, heads - 1)], kv_send.at[turn])


def solution(mesh):
    heads = mesh.shape["head"]
    chips = heads // 2

    def shards(entering, fresh_slice, norm_gain, w_query, w_key_value, doc_lengths):
        _, tokens, width = entering.shape
        features = w_query.shape[1]
        columns = w_key_value.shape[2]
        docs = doc_lengths.shape[0]
        any_spec = pl.BlockSpec(memory_space=pl.ANY)
        dma = pltpu.SemaphoreType.DMA
        vmem = pltpu.VMEM
        out = pl.pallas_call(
            body,
            out_shape=jax.ShapeDtypeStruct((tokens, width), BF16),
            in_specs=[any_spec] * 6,
            out_specs=pl.BlockSpec(memory_space=pltpu.VMEM),
            scratch_shapes=[
                vmem((2, chips, tokens, width), BF16),
                vmem((tokens, features // 2), BF16),
                vmem((2, chips, width, width), BF16),
                vmem((2, chips, columns, width), BF16),
                vmem((chips, 2 * columns, width), BF16),
                vmem((1, features), F32),
                vmem((1, docs), jnp.int32),
                vmem((1, 128), F32),
                vmem((tokens, width), BF16),
                vmem((tokens, width), BF16),
                vmem((2, KVH, 16, tokens), BF16),
                vmem((2, heads, 16, tokens), BF16),
                vmem((2 * columns, tokens), F32),
                vmem((tokens, 128), F32),
                vmem((2, columns + 8, tokens), F32),
                vmem((2, columns + 8, tokens), F32),
                vmem((2, tokens, width), F32),
                vmem((2, tokens, width), F32),
                vmem((tokens, tokens), F32),
                vmem((tokens, 2 * tokens), F32),
                dma((5,)),
                dma,
                dma((2,)),
                dma((2,)),
                dma((2, 2, 5, PIECES)),
                dma((2,)),
                dma,
                dma((2,)),
                dma((2,)),
                dma((2,)),
                dma((2,)),
                dma((2,)),
                dma((2,)),
                dma((2,)),
            ],
            compiler_params=pltpu.CompilerParams(collective_id=0, has_side_effects=True),
        )(
            entering[0], fresh_slice, norm_gain, w_query[0].reshape(chips, 2, width, width),
            w_key_value[0].T, doc_lengths.reshape(1, docs),
        )
        return out[None]

    placed = (
        P("section", None, "head"),
        P(None, "head"),
        P("section", None),
        P("section", None, "head"),
        P("section", None, "head"),
        P(),
    )
    return jax.shard_map(
        shards, mesh=mesh, in_specs=placed, out_specs=P("section", None, "head"), check_vma=False
    )
```

```python
import functools
import math

import jax
import jax.numpy as jnp
from jax import lax
from jax.experimental import pallas as pl
from jax.experimental.pallas import tpu as pltpu
from jax.sharding import PartitionSpec as P

MESH = pl.DeviceIdType.MESH
HD = 128
KVH = 4
GROUP = 8
EPS = 1e-05
NEG = -1e30
PIECES = 4
F32 = jnp.float32
BF16 = jnp.bfloat16
NT = (((1,), (1,)), ((), ()))


def iota(shape, dim):
    return lax.broadcasted_iota(jnp.int32, shape, dim)


def body(
    x_hbm, fresh_hbm, gain_hbm, wq_hbm, wkv_hbm, len_hbm, out_ref,
    xg, xn, wq, wkv_raw, wkv, gain, lens, lens_pad, fresh, first, kvst, kvbuf,
    acc, sq, part_out, part_in, query_out, query_in, bias1, bias2,
    load_sem, own_sem, swap_send, swap_recv, ring_recv, ring_send, hop_send,
    part_send, part_recv, query_send, query_recv, kv_recv, kv_send, kv_own,
):
    sections = lax.axis_size("section")
    heads = lax.axis_size("head")
    chips = heads // 2
    tokens, width = first.shape
    columns = wkv_hbm.shape[0]
    rows = tokens // PIECES
    here = width // HD
    s = lax.axis_index("section")
    h = lax.axis_index("head")
    y, core = h // 2, h % 2
    mate = (s, y * 2 + (1 - core))
    following = ((s + 1) % sections, h)
    previous = ((s + sections - 1) % sections, h)

    def chip(offset):
        return (y + offset + chips) % chips

    def peer(offset):
        return (s, chip(offset) * 2 + core)

    def send(src, dst, send_sem, recv_sem, device):
        pltpu.make_async_remote_copy(
            src_ref=src, dst_ref=dst, send_sem=send_sem, recv_sem=recv_sem,
            device_id=device, device_id_type=MESH,
        ).start()

    def await_recv(ref, sem):
        pltpu.make_async_remote_copy(
            src_ref=ref, dst_ref=ref, send_sem=sem, recv_sem=sem,
            device_id=mate, device_id_type=MESH,
        ).wait_recv()

    def await_send(ref, sem):
        pltpu.make_async_remote_copy(
            src_ref=ref, dst_ref=ref, send_sem=sem, recv_sem=sem,
            device_id=mate, device_id_type=MESH,
        ).wait_send()

    def piece(p):
        return pl.ds(p * rows, rows)

    barrier = pltpu.get_barrier_semaphore()
    greeted = [mate, peer(1), peer(-1), peer(2), peer(-2), previous]
    for device in greeted:
        pl.semaphore_signal(barrier, inc=1, device_id=device, device_id_type=MESH)

    own = pltpu.make_async_copy(x_hbm, xg.at[0, y], own_sem)
    own.start()
    loads = [
        pltpu.make_async_copy(src, dst, load_sem.at[i])
        for i, (src, dst) in enumerate(
            ((gain_hbm, gain), (len_hbm, lens), (fresh_hbm, fresh), (wq_hbm.at[:, core], wq.at[0]))
        )
    ]
    for load in loads:
        load.start()

    def lanes(k, parity):
        return pl.ds(pl.multiple_of((2 * k + parity) * width, width), width)

    for k in range(chips):
        pltpu.make_async_copy(
            wkv_hbm.at[:, lanes(k, core)], wkv_raw.at[0, k], load_sem.at[4]
        ).start()
    pl.semaphore_wait(barrier, len(greeted))

    half = chips // 2
    halves = (range(0, PIECES // 2), range(PIECES // 2, PIECES))
    sides = ((0, 1), (1, -1))
    passed_by = {1: 0, 2: 0, 3: 2, 4: 2}

    def pieces(k, d):
        return range(PIECES) if k < half else halves[d]

    def pass_on(turn, k, p, d, src=None):
        sign = sides[d][1]
        owner = chip(-sign * k)
        chunk = xg.at[turn, owner, piece(p)]
        for k2 in (4, 3, 2, 1):
            if passed_by[k2] == k and k2 > k and p in pieces(k2, d):
                send(chunk if src is None else src, chunk, ring_send.at[turn],
                     ring_recv.at[turn, d, k2, p], peer(sign * (k2 - k)))

    def await_ring(turn, k):
        for p in range(PIECES):
            for d, sign in sides:
                if p in pieces(k, d):
                    await_recv(xg.at[turn, chip(-sign * k), piece(p)], ring_recv.at[turn, d, k, p])
                    pass_on(turn, k, p, d)

    def swap_weights():
        for k in range(chips):
            send(wkv_hbm.at[:, lanes(k, 1 - core)], wkv_raw.at[1, k], swap_send.at[0],
                 swap_recv.at[0], mate)
        send(wq_hbm.at[:, 1 - core], wq.at[1], swap_send.at[1], swap_recv.at[1], mate)

    def masks():
        for load in loads[1:3]:
            load.wait()
        docs = lens.shape[1]
        lens_pad[...] = jnp.zeros_like(lens_pad)
        lens_pad[:, 0:docs] = lens[...].astype(F32)
        n = lens_pad.shape[1]
        e0, e1 = iota((n, n), 0), iota((n, n), 1)
        row = jnp.broadcast_to(lens_pad[...], (n, n))
        far = F32(1e9)
        ends_col = jnp.sum(jnp.where(e1 <= e0, row, 0.0), axis=1, keepdims=True)
        ends_col = jnp.where(iota((n, 1), 0) < docs, ends_col, far)
        ends_row = jnp.sum(jnp.where(e0 == e1, ends_col, 0.0), axis=0, keepdims=True)
        start = ((sections - 1 - s) * tokens).astype(F32)

        def docs_of_rows(begin):
            pos = begin + iota((tokens, n), 0).astype(F32)
            return jnp.sum((ends_row <= pos).astype(F32), axis=1, keepdims=True)

        def docs_of_columns(begin):
            pos = begin + iota((n, tokens), 1).astype(F32)
            return jnp.sum((ends_col <= pos).astype(F32), axis=0, keepdims=True)

        q1, q2 = docs_of_rows(start), docs_of_rows(start + tokens)
        k1, k2 = docs_of_columns(start), docs_of_columns(start + tokens)
        causal = iota((tokens, tokens), 1) <= iota((tokens, tokens), 0)
        bias1[...] = jnp.where(causal & (q1 == k1), 0.0, NEG)
        bias2[:, 0:tokens] = jnp.where(q2 == k1, 0.0, NEG)
        bias2[:, tokens:2 * tokens] = jnp.where(causal & (q2 == k2), 0.0, NEG)
    def order_columns():
        r, c = iota((columns, columns), 0), iota((columns, columns), 1)
        perm = (((c % 8) // 2 == r // 16) & (c // 8 == r % 8) & (c % 2 == (r % 16) // 8))
        perm = perm.astype(F32).astype(BF16)
        loads[0].wait()
        pltpu.make_async_copy(wkv_raw.at[0], wkv_raw.at[0], load_sem.at[4]).wait()
        await_recv(wkv_raw.at[1], swap_recv.at[0])
        for k in range(chips):
            for side in range(2):
                wkv[k, side * columns:(side + 1) * columns] = jnp.dot(
                    perm, wkv_raw[side, k], preferred_element_type=F32
                ).astype(BF16)

    def clear():
        acc[...] = jnp.zeros_like(acc)
        sq[...] = jnp.zeros_like(sq)

    def take(turn, offset):
        k = chip(offset)
        wide = xg[turn, k].astype(F32)
        low, high = wide[:, 0:128], wide[:, 128:256]
        sq[...] += low * low + high * high
        scaled = (wide * gain[:, lanes(k, core)]).astype(BF16)
        xn[:, pl.ds(pl.multiple_of(k * width, width), width)] = scaled
        acc[...] += lax.dot_general(wkv[k], scaled, NT, preferred_element_type=F32)

    def take_both(turn, k):
        take(turn, -k)
        if k < half:
            take(turn, k)

    group = h * here // GROUP
    sel_r, sel_c = iota((HD, 2 * HD), 0), iota((HD, 2 * HD), 1)
    same_peer = sel_r // 8 == sel_c // 16
    pick_key = (same_peer & (sel_c % 16 == sel_r % 8)).astype(F32).astype(BF16)
    pick_value = (same_peer & (sel_c % 16 == 8 + sel_r % 8)).astype(F32).astype(BF16)
    diag = iota((tokens, tokens), 0) == iota((tokens, tokens), 1)

    def exchange(turn):
        square = jnp.sum(sq[...], axis=1, keepdims=True)
        square = jnp.sum(jnp.where(diag, square, 0.0), axis=0, keepdims=True)
        part_out[turn, 0:columns] = acc[columns:2 * columns]
        part_out[turn, columns:columns + 8] = jnp.broadcast_to(square, (8, tokens))
        send(part_out.at[turn], part_in.at[turn], part_send.at[turn], part_recv.at[turn], mate)
        await_recv(part_in.at[turn], part_recv.at[turn])
        square = square + part_in[turn, columns:columns + 1]
        scale = lax.rsqrt(square * (1.0 / (heads * width)) + EPS)
        total = acc[0:columns] + part_in[turn, 0:columns]
        kvst[turn] = (total * scale).astype(BF16).reshape(KVH, 16, tokens)
        far_first = sorted(range(1 - half, half + 1), key=abs, reverse=True)
        others = [chip(far) * 2 + side for far in far_first if far for side in (core, 1 - core)]
        for other in others + [y * 2 + 1 - core]:
            send(kvst.at[turn, other * here // GROUP], kvbuf.at[turn, h],
                 kv_send.at[turn], kv_recv.at[turn], (s, other))
        keep = pltpu.make_async_copy(kvst.at[turn, group], kvbuf.at[turn, h], kv_own.at[turn])
        keep.start()
        return scale, keep

    def queries(turn, scale):
        def product(side):
            w = wq[side].reshape(chips * width, width)
            return jnp.dot(xn[...], w, preferred_element_type=F32)

        query_out[turn] = product(1)
        send(query_out.at[turn], query_in.at[turn], query_send.at[turn], query_recv.at[turn], mate)
        q = product(0)
        scale = jnp.sum(jnp.where(diag, scale, 0.0), axis=1, keepdims=True)
        await_recv(query_in.at[turn], query_recv.at[turn])
        q = ((q + query_in[turn]) * scale).astype(BF16)
        spread = [
            jnp.dot(q[:, i * HD:(i + 1) * HD], pick_key, preferred_element_type=F32)
            for i in range(here)
        ]
        return jnp.concatenate(spread, axis=0).astype(BF16)

    def await_kv(turn, keep):
        keep.wait()
        await_recv(kvbuf.at[turn, pl.ds(0, heads - 1)], kv_recv.at[turn])

    def attend(turn, wide_q, bias):
        both = [kvbuf[t].reshape(heads * 16, tokens) for t in range(turn + 1)]
        scores = [
            jnp.dot(wide_q, kv, preferred_element_type=F32) * (1.0 / math.sqrt(HD)) for kv in both
        ]
        scores = jnp.concatenate(scores, axis=1) + jnp.concatenate([bias[...]] * here, axis=0)
        expon = jnp.exp(scores - jnp.max(scores, axis=1, keepdims=True))
        weights = (expon / jnp.sum(expon, axis=1, keepdims=True)).astype(BF16)
        values = [
            jnp.dot(pick_value, kv, preferred_element_type=F32).astype(BF16) for kv in both
        ]
        values = jnp.concatenate(values, axis=1)
        mixed = lax.dot_general(weights, values, NT, preferred_element_type=F32).astype(BF16)
        mixed = mixed.astype(F32)
        for i in range(here):
            cols = slice(i * HD, (i + 1) * HD)
            total = xg[turn, y, :, cols].astype(F32) + mixed[i * tokens:(i + 1) * tokens]
            if turn == 0:
                total = jnp.where(s == sections - 1, fresh[:, cols].astype(F32), total)
                first[:, cols] = total.astype(BF16)
            else:
                out_ref[:, cols] = total.astype(BF16)

    def rest_of_gather(turn):
        await_ring(turn, 2)
        if turn == 0:
            order_columns()
            own.wait()
        take(turn, 0)
        await_ring(turn, 1)
        take_both(turn, 1)
        take_both(turn, 2)
        await_ring(turn, 3)
        take_both(turn, 3)
        await_ring(turn, 4)
        take_both(turn, 4)

    for p in range(PIECES):
        for d, _ in sides:
            pass_on(0, 0, p, d, x_hbm.at[piece(p)])
    swap_weights()
    clear()
    rest_of_gather(0)
    scale, keep = exchange(0)
    loads[3].wait()
    await_recv(wq.at[1], swap_recv.at[1])
    wide_q = queries(0, scale)
    masks()
    await_kv(0, keep)
    attend(0, wide_q, bias1)

    for p in range(PIECES):
        send(first.at[piece(p)], xg.at[1, y, piece(p)], hop_send, ring_recv.at[1, 0, 0, p], following)

    clear()
    for p in range(PIECES):
        await_recv(xg.at[1, y, piece(p)], ring_recv.at[1, 0, 0, p])
        for d, _ in sides:
            pass_on(1, 0, p, d)
    rest_of_gather(1)
    scale, keep = exchange(1)
    wide_q = queries(1, scale)
    await_kv(1, keep)
    attend(1, wide_q, bias2)

    await_send(first, hop_send)
    await_send(wkv_raw.at[1], swap_send.at[0])
    await_send(wq.at[1], swap_send.at[1])
    for turn in range(2):
        await_send(xg.at[turn, pl.ds(0, 2 * half - 1)], ring_send.at[turn])
        await_send(part_out.at[turn], part_send.at[turn])
        await_send(query_out.at[turn], query_send.at[turn])
        await_send(kvbuf.at[turn, pl.ds(0, heads - 1)], kv_send.at[turn])


def solution(mesh):
    heads = mesh.shape["head"]
    chips = heads // 2

    def shards(entering, fresh_slice, norm_gain, w_query, w_key_value, doc_lengths):
        _, tokens, width = entering.shape
        features = w_query.shape[1]
        columns = w_key_value.shape[2]
        docs = doc_lengths.shape[0]
        any_spec = pl.BlockSpec(memory_space=pl.ANY)
        dma = pltpu.SemaphoreType.DMA
        vmem = pltpu.VMEM
        out = pl.pallas_call(
            body,
            out_shape=pltpu.VMEM((tokens, width), BF16),
            in_specs=[any_spec] * 6,
            out_specs=pl.BlockSpec(memory_space=pltpu.VMEM),
            scratch_shapes=[
                vmem((2, chips, tokens, width), BF16),
                vmem((tokens, features // 2), BF16),
                vmem((2, chips, width, width), BF16),
                vmem((2, chips, columns, width), BF16),
                vmem((chips, 2 * columns, width), BF16),
                vmem((1, features), F32),
                vmem((1, docs), jnp.int32),
                vmem((1, 128), F32),
                vmem((tokens, width), BF16),
                vmem((tokens, width), BF16),
                vmem((2, KVH, 16, tokens), BF16),
                vmem((2, heads, 16, tokens), BF16),
                vmem((2 * columns, tokens), F32),
                vmem((tokens, 128), F32),
                vmem((2, columns + 8, tokens), F32),
                vmem((2, columns + 8, tokens), F32),
                vmem((2, tokens, width), F32),
                vmem((2, tokens, width), F32),
                vmem((tokens, tokens), F32),
                vmem((tokens, 2 * tokens), F32),
                dma((5,)),
                dma,
                dma((2,)),
                dma((2,)),
                dma((2, 2, 5, PIECES)),
                dma((2,)),
                dma,
                dma((2,)),
                dma((2,)),
                dma((2,)),
                dma((2,)),
                dma((2,)),
                dma((2,)),
                dma((2,)),
            ],
            compiler_params=pltpu.CompilerParams(collective_id=0, has_side_effects=True),
        )(
            entering[0], fresh_slice, norm_gain, w_query[0].reshape(chips, 2, width, width),
            w_key_value[0].T, doc_lengths.reshape(1, docs),
        )
        return out[None]

    placed = (
        P("section", None, "head"),
        P(None, "head"),
        P("section", None),
        P("section", None, "head"),
        P("section", None, "head"),
        P(),
    )
    return jax.shard_map(
        shards, mesh=mesh, in_specs=placed, out_specs=P("section", None, "head"), check_vma=False
    )
```

```python
import functools
import math

import jax
import jax.numpy as jnp
from jax import lax
from jax.experimental import pallas as pl
from jax.experimental.pallas import tpu as pltpu
from jax.sharding import PartitionSpec as P

MESH = pl.DeviceIdType.MESH
HD = 128
KVH = 4
GROUP = 8
EPS = 1e-05
NEG = -1e30
PIECES = 4
LINE = 8
F32 = jnp.float32
BF16 = jnp.bfloat16
NT = (((1,), (1,)), ((), ()))


def iota(shape, dim):
    return lax.broadcasted_iota(jnp.int32, shape, dim)


def body(
    x_hbm, fresh_hbm, gain_hbm, wq_hbm, wkv_hbm, len_hbm, out_ref,
    xg, xn, wq, wkv_raw, wkv, wkv_quad, gain, lens, lens_pad, fresh, first, kvst, kvbuf,
    acc, sq, part_out, part_in, query_out, query_in, bias1, bias2,
    load_sem, own_sem, swap_send, swap_recv, ring_recv, ring_send, hop_send,
    part_send, part_recv, query_send, query_recv, kv_recv, kv_send, kv_own,
    quad_send, quad_recv,
):
    sections = lax.axis_size("section")
    heads = lax.axis_size("head")
    chips = heads // 2
    tokens, width = first.shape
    columns = wkv_hbm.shape[0]
    rows = tokens // PIECES
    here = width // HD
    s = lax.axis_index("section")
    h = lax.axis_index("head")
    y, core = h // 2, h % 2
    mate = (s, y * 2 + (1 - core))
    following = ((s + 1) % sections, h)
    previous = ((s + sections - 1) % sections, h)

    def chip(offset):
        return (y + offset + chips) % chips

    def peer(offset):
        return (s, chip(offset) * 2 + core)

    def send(src, dst, send_sem, recv_sem, device):
        pltpu.make_async_remote_copy(
            src_ref=src, dst_ref=dst, send_sem=send_sem, recv_sem=recv_sem,
            device_id=device, device_id_type=MESH,
        ).start()

    def await_recv(ref, sem):
        pltpu.make_async_remote_copy(
            src_ref=ref, dst_ref=ref, send_sem=sem, recv_sem=sem,
            device_id=mate, device_id_type=MESH,
        ).wait_recv()

    def await_send(ref, sem):
        pltpu.make_async_remote_copy(
            src_ref=ref, dst_ref=ref, send_sem=sem, recv_sem=sem,
            device_id=mate, device_id_type=MESH,
        ).wait_send()

    def piece(p):
        return pl.ds(p * rows, rows)

    barrier = pltpu.get_barrier_semaphore()
    greeted = [mate, peer(1), peer(-1), peer(2), peer(-2), previous]
    for device in greeted:
        pl.semaphore_signal(barrier, inc=1, device_id=device, device_id_type=MESH)

    own = pltpu.make_async_copy(x_hbm, xg.at[0, y], own_sem)
    own.start()
    loads = [
        pltpu.make_async_copy(src, dst, load_sem.at[i])
        for i, (src, dst) in enumerate(
            ((gain_hbm, gain), (len_hbm, lens), (fresh_hbm, fresh), (wq_hbm.at[:, core], wq.at[0]))
        )
    ]
    for load in loads:
        load.start()

    def lanes(k, parity):
        return pl.ds(pl.multiple_of((2 * k + parity) * width, width), width)

    for k in range(chips):
        pltpu.make_async_copy(
            wkv_hbm.at[:, lanes(k, core)], wkv_raw.at[0, k], load_sem.at[4]
        ).start()
    pl.semaphore_wait(barrier, len(greeted))

    half = chips // 2
    halves = (range(0, PIECES // 2), range(PIECES // 2, PIECES))
    sides = ((0, 1), (1, -1))
    passed_by = {1: 0, 2: 0, 3: 2, 4: 2}

    def pieces(k, d):
        return range(PIECES) if k < half else halves[d]

    def pass_on(turn, k, p, d, src=None):
        sign = sides[d][1]
        owner = chip(-sign * k)
        chunk = xg.at[turn, owner, piece(p)]
        for k2 in (4, 3, 2, 1):
            if passed_by[k2] == k and k2 > k and p in pieces(k2, d):
                send(chunk if src is None else src, chunk, ring_send.at[turn],
                     ring_recv.at[turn, d, k2, p], peer(sign * (k2 - k)))

    def await_ring(turn, k):
        for p in range(PIECES):
            for d, sign in sides:
                if p in pieces(k, d):
                    await_recv(xg.at[turn, chip(-sign * k), piece(p)], ring_recv.at[turn, d, k, p])
                    pass_on(turn, k, p, d)

    def swap_weights():
        for k in range(chips):
            send(wkv_hbm.at[:, lanes(k, 1 - core)], wkv_raw.at[1, k], swap_send.at[0],
                 swap_recv.at[0], mate)
        send(wq_hbm.at[:, 1 - core], wq.at[1], swap_send.at[1], swap_recv.at[1], mate)

    def masks():
        for load in loads[1:3]:
            load.wait()
        docs = lens.shape[1]
        lens_pad[...] = jnp.zeros_like(lens_pad)
        lens_pad[:, 0:docs] = lens[...].astype(F32)
        n = lens_pad.shape[1]
        e0, e1 = iota((n, n), 0), iota((n, n), 1)
        row = jnp.broadcast_to(lens_pad[...], (n, n))
        far = F32(1e9)
        ends_col = jnp.sum(jnp.where(e1 <= e0, row, 0.0), axis=1, keepdims=True)
        ends_col = jnp.where(iota((n, 1), 0) < docs, ends_col, far)
        ends_row = jnp.sum(jnp.where(e0 == e1, ends_col, 0.0), axis=0, keepdims=True)
        start = ((sections - 1 - s) * tokens).astype(F32)

        def docs_of_rows(begin):
            pos = begin + iota((tokens, n), 0).astype(F32)
            return jnp.sum((ends_row <= pos).astype(F32), axis=1, keepdims=True)

        def docs_of_columns(begin):
            pos = begin + iota((n, tokens), 1).astype(F32)
            return jnp.sum((ends_col <= pos).astype(F32), axis=0, keepdims=True)

        q1, q2 = docs_of_rows(start), docs_of_rows(start + tokens)
        k1, k2 = docs_of_columns(start), docs_of_columns(start + tokens)
        causal = iota((tokens, tokens), 1) <= iota((tokens, tokens), 0)
        bias1[...] = jnp.where(causal & (q1 == k1), 0.0, NEG)
        bias2[:, 0:tokens] = jnp.where(q2 == k1, 0.0, NEG)
        bias2[:, tokens:2 * tokens] = jnp.where(causal & (q2 == k2), 0.0, NEG)
    def order_columns():
        r, c = iota((columns, columns), 0), iota((columns, columns), 1)
        perm = (((c % 8) // 2 == r // 16) & (c // 8 == r % 8) & (c % 2 == (r % 16) // 8))
        perm = perm.astype(F32).astype(BF16)
        loads[0].wait()
        pltpu.make_async_copy(wkv_raw.at[0], wkv_raw.at[0], load_sem.at[4]).wait()
        await_recv(wkv_raw.at[1], swap_recv.at[0])
        for k in range(chips):
            for side in range(2):
                wkv[k, side * columns:(side + 1) * columns] = jnp.dot(
                    perm, wkv_raw[side, k], preferred_element_type=F32
                ).astype(BF16)

    def clear():
        acc[...] = jnp.zeros_like(acc)
        sq[...] = jnp.zeros_like(sq)

    def take(turn, offset):
        k = chip(offset)
        wide = xg[turn, k].astype(F32)
        low, high = wide[:, 0:128], wide[:, 128:256]
        sq[...] += low * low + high * high
        scaled = (wide * gain[:, lanes(k, core)]).astype(BF16)
        xn[:, pl.ds(pl.multiple_of(k * width, width), width)] = scaled
        w = wkv[k] if turn == 0 else wkv_quad[k].reshape(2 * columns, width)
        acc[...] += lax.dot_general(w, scaled, NT, preferred_element_type=F32)

    def take_both(turn, k):
        take(turn, -k)
        if k < half:
            take(turn, k)

    group = h * here // GROUP
    sel_r, sel_c = iota((HD, 2 * HD), 0), iota((HD, 2 * HD), 1)
    same_peer = sel_r // 8 == sel_c // 16
    pick_key = (same_peer & (sel_c % 16 == sel_r % 8)).astype(F32).astype(BF16)
    pick_value = (same_peer & (sel_c % 16 == 8 + sel_r % 8)).astype(F32).astype(BF16)
    diag = iota((tokens, tokens), 0) == iota((tokens, tokens), 1)

    def share_out(act):
        part = y % half
        for m in range(KVH):
            target = 2 * m + y // half
            for side, at in ((0, core), (1, 1 - core)):
                slot = ((part // 2 + core) % 2) * 4 + (part % 2) * 2 + at
                rows_of = pl.ds(side * columns + m * 16, 16)
                act(target, wkv.at[:, rows_of], wkv_quad.at[:, slot])

    def start_share(target, src, dst):
        @pl.when(target == y)
        def _():
            pltpu.make_async_copy(src, dst, quad_recv).start()

        @pl.when(target != y)
        def _():
            send(src, dst, quad_send, quad_recv, (s, target * 2 + core))

    early = s % LINE == 0

    def share():
        share_out(start_share)

    def exchange(turn):
        square = jnp.sum(sq[...], axis=1, keepdims=True)
        square = jnp.sum(jnp.where(diag, square, 0.0), axis=0, keepdims=True)
        part_out[turn, 0:columns] = acc[columns:2 * columns]
        part_out[turn, columns:columns + 8] = jnp.broadcast_to(square, (8, tokens))
        send(part_out.at[turn], part_in.at[turn], part_send.at[turn], part_recv.at[turn], mate)
        await_recv(part_in.at[turn], part_recv.at[turn])
        square = square + part_in[turn, columns:columns + 1]
        scale = lax.rsqrt(square * (1.0 / (heads * width)) + EPS)
        total = acc[0:columns] + part_in[turn, 0:columns]
        kvst[turn] = (total * scale).astype(BF16).reshape(KVH, 16, tokens)
        if turn == 1:
            quad = h // KVH * KVH
            mine = kvbuf.at[1, pl.ds(h % KVH * KVH, KVH)]
            for d in (2, 3, 1):
                send(kvst.at[1], mine, kv_send.at[1], kv_recv.at[1], (s, quad + (h + d) % KVH))
            keep = pltpu.make_async_copy(kvst.at[1], mine, kv_own.at[1])
            keep.start()
            return scale, keep
        far_first = sorted(range(1 - half, half + 1), key=abs, reverse=True)
        others = [chip(far) * 2 + side for far in far_first if far for side in (core, 1 - core)]
        for other in others + [y * 2 + 1 - core]:
            send(kvst.at[turn, other * here // GROUP], kvbuf.at[turn, h],
                 kv_send.at[turn], kv_recv.at[turn], (s, other))
        keep = pltpu.make_async_copy(kvst.at[turn, group], kvbuf.at[turn, h], kv_own.at[turn])
        keep.start()
        return scale, keep

    def queries(turn, scale):
        def product(side):
            w = wq[side].reshape(chips * width, width)
            return jnp.dot(xn[...], w, preferred_element_type=F32)

        query_out[turn] = product(1)
        send(query_out.at[turn], query_in.at[turn], query_send.at[turn], query_recv.at[turn], mate)
        q = product(0)
        scale = jnp.sum(jnp.where(diag, scale, 0.0), axis=1, keepdims=True)
        await_recv(query_in.at[turn], query_recv.at[turn])
        q = ((q + query_in[turn]) * scale).astype(BF16)
        spread = [
            jnp.dot(q[:, i * HD:(i + 1) * HD], pick_key, preferred_element_type=F32)
            for i in range(here)
        ]
        return jnp.concatenate(spread, axis=0).astype(BF16)

    kv_count = (heads - 1, heads - KVH)

    def await_kv(turn, keep):
        keep.wait()
        await_recv(kvbuf.at[turn, pl.ds(0, kv_count[turn])], kv_recv.at[turn])

    def attend(turn, wide_q, bias):
        both = [kvbuf[t].reshape(heads * 16, tokens) for t in range(turn + 1)]
        scores = [
            jnp.dot(wide_q, kv, preferred_element_type=F32) * (1.0 / math.sqrt(HD)) for kv in both
        ]
        scores = jnp.concatenate(scores, axis=1) + jnp.concatenate([bias[...]] * here, axis=0)
        expon = jnp.exp(scores - jnp.max(scores, axis=1, keepdims=True))
        weights = (expon / jnp.sum(expon, axis=1, keepdims=True)).astype(BF16)
        values = [
            jnp.dot(pick_value, kv, preferred_element_type=F32).astype(BF16) for kv in both
        ]
        values = jnp.concatenate(values, axis=1)
        mixed = lax.dot_general(weights, values, NT, preferred_element_type=F32).astype(BF16)
        mixed = mixed.astype(F32)
        for i in range(here):
            cols = slice(i * HD, (i + 1) * HD)
            total = xg[turn, y, :, cols].astype(F32) + mixed[i * tokens:(i + 1) * tokens]
            if turn == 0:
                total = jnp.where(s == sections - 1, fresh[:, cols].astype(F32), total)
                first[:, cols] = total.astype(BF16)
            else:
                out_ref[:, cols] = total.astype(BF16)

    def rest_of_gather(turn):
        await_ring(turn, 2)
        if turn == 0:
            order_columns()
            pl.when(early)(share)
            own.wait()
        else:
            await_recv(wkv_quad, quad_recv)
        take(turn, 0)
        await_ring(turn, 1)
        take_both(turn, 1)
        take_both(turn, 2)
        await_ring(turn, 3)
        take_both(turn, 3)
        await_ring(turn, 4)
        take_both(turn, 4)

    for p in range(PIECES):
        for d, _ in sides:
            pass_on(0, 0, p, d, x_hbm.at[piece(p)])
    swap_weights()
    clear()
    rest_of_gather(0)
    scale, keep = exchange(0)
    loads[3].wait()
    await_recv(wq.at[1], swap_recv.at[1])
    wide_q = queries(0, scale)
    masks()
    await_kv(0, keep)
    attend(0, wide_q, bias1)

    for p in range(PIECES):
        send(first.at[piece(p)], xg.at[1, y, piece(p)], hop_send, ring_recv.at[1, 0, 0, p], following)

    pl.when(jnp.logical_not(early))(share)

    clear()
    for p in range(PIECES):
        await_recv(xg.at[1, y, piece(p)], ring_recv.at[1, 0, 0, p])
        for d, _ in sides:
            pass_on(1, 0, p, d)
    rest_of_gather(1)
    scale, keep = exchange(1)
    wide_q = queries(1, scale)
    await_kv(1, keep)
    attend(1, wide_q, bias2)

    await_send(first, hop_send)
    keeps = y % 2 == y // half

    @pl.when(keeps)
    def _():
        await_send(wkv_quad.at[:, 0:2 * (KVH - 1)], quad_send)

    @pl.when(jnp.logical_not(keeps))
    def _():
        await_send(wkv_quad, quad_send)

    await_send(wkv_raw.at[1], swap_send.at[0])
    await_send(wq.at[1], swap_send.at[1])
    for turn in range(2):
        await_send(xg.at[turn, pl.ds(0, 2 * half - 1)], ring_send.at[turn])
        await_send(part_out.at[turn], part_send.at[turn])
        await_send(query_out.at[turn], query_send.at[turn])
        await_send(kvbuf.at[turn, pl.ds(0, kv_count[turn])], kv_send.at[turn])


def solution(mesh):
    heads = mesh.shape["head"]
    chips = heads // 2

    def shards(entering, fresh_slice, norm_gain, w_query, w_key_value, doc_lengths):
        _, tokens, width = entering.shape
        features = w_query.shape[1]
        columns = w_key_value.shape[2]
        docs = doc_lengths.shape[0]
        any_spec = pl.BlockSpec(memory_space=pl.ANY)
        dma = pltpu.SemaphoreType.DMA
        vmem = pltpu.VMEM
        out = pl.pallas_call(
            body,
            out_shape=pltpu.VMEM((tokens, width), BF16),
            in_specs=[any_spec] * 6,
            out_specs=pl.BlockSpec(memory_space=pltpu.VMEM),
            scratch_shapes=[
                vmem((2, chips, tokens, width), BF16),
                vmem((tokens, features // 2), BF16),
                vmem((2, chips, width, width), BF16),
                vmem((2, chips, columns, width), BF16),
                vmem((chips, 2 * columns, width), BF16),
                vmem((chips, 2 * KVH, 16, width), BF16),
                vmem((1, features), F32),
                vmem((1, docs), jnp.int32),
                vmem((1, 128), F32),
                vmem((tokens, width), BF16),
                vmem((tokens, width), BF16),
                vmem((2, KVH, 16, tokens), BF16),
                vmem((2, heads, 16, tokens), BF16),
                vmem((2 * columns, tokens), F32),
                vmem((tokens, 128), F32),
                vmem((2, columns + 8, tokens), F32),
                vmem((2, columns + 8, tokens), F32),
                vmem((2, tokens, width), F32),
                vmem((2, tokens, width), F32),
                vmem((tokens, tokens), F32),
                vmem((tokens, 2 * tokens), F32),
                dma((5,)),
                dma,
                dma((2,)),
                dma((2,)),
                dma((2, 2, 5, PIECES)),
                dma((2,)),
                dma,
                dma((2,)),
                dma((2,)),
                dma((2,)),
                dma((2,)),
                dma((2,)),
                dma((2,)),
                dma((2,)),
                dma,
                dma,
            ],
            compiler_params=pltpu.CompilerParams(collective_id=0, has_side_effects=True),
        )(
            entering[0], fresh_slice, norm_gain, w_query[0].reshape(chips, 2, width, width),
            w_key_value[0].T, doc_lengths.reshape(1, docs),
        )
        return out[None]

    placed = (
        P("section", None, "head"),
        P(None, "head"),
        P("section", None),
        P("section", None, "head"),
        P("section", None, "head"),
        P(),
    )
    return jax.shard_map(
        shards, mesh=mesh, in_specs=placed, out_specs=P("section", None, "head"), check_vma=False
    )
```

```python
import functools
import math

import jax
import jax.numpy as jnp
from jax import lax
from jax.experimental import pallas as pl
from jax.experimental.pallas import tpu as pltpu
from jax.sharding import PartitionSpec as P

MESH = pl.DeviceIdType.MESH
HD = 128
KVH = 4
GROUP = 8
EPS = 1e-05
NEG = -1e30
PIECES = 4
LINE = 8
F32 = jnp.float32
BF16 = jnp.bfloat16
NT = (((1,), (1,)), ((), ()))


def iota(shape, dim):
    return lax.broadcasted_iota(jnp.int32, shape, dim)


def body(
    x_hbm, fresh_hbm, gain_hbm, wq_hbm, wkv_hbm, len_hbm, out_ref,
    xg, xn, wq, wkv_raw, wkv, wkv_quad, gain, lens, lens_pad, fresh, first, kvst, kvbuf,
    acc, sq, part_out, part_in, query_out, query_in, bias1, bias2,
    load_sem, own_sem, swap_send, swap_recv, ring_recv, ring_send, hop_send,
    part_send, part_recv, query_send, query_recv, kv_recv, kv_send, kv_own,
    quad_send, quad_recv,
):
    sections = lax.axis_size("section")
    heads = lax.axis_size("head")
    chips = heads // 2
    tokens, width = first.shape
    columns = wkv_hbm.shape[0]
    rows = tokens // PIECES
    here = width // HD
    s = lax.axis_index("section")
    h = lax.axis_index("head")
    y, core = h // 2, h % 2
    mate = (s, y * 2 + (1 - core))
    following = ((s + 1) % sections, h)
    previous = ((s + sections - 1) % sections, h)

    def chip(offset):
        return (y + offset + chips) % chips

    def peer(offset):
        return (s, chip(offset) * 2 + core)

    def send(src, dst, send_sem, recv_sem, device):
        pltpu.make_async_remote_copy(
            src_ref=src, dst_ref=dst, send_sem=send_sem, recv_sem=recv_sem,
            device_id=device, device_id_type=MESH,
        ).start()

    def await_recv(ref, sem):
        pltpu.make_async_remote_copy(
            src_ref=ref, dst_ref=ref, send_sem=sem, recv_sem=sem,
            device_id=mate, device_id_type=MESH,
        ).wait_recv()

    def await_send(ref, sem):
        pltpu.make_async_remote_copy(
            src_ref=ref, dst_ref=ref, send_sem=sem, recv_sem=sem,
            device_id=mate, device_id_type=MESH,
        ).wait_send()

    def piece(p):
        return pl.ds(p * rows, rows)

    barrier = pltpu.get_barrier_semaphore()
    greeted = [mate, peer(1), peer(-1), peer(2), peer(-2), previous]
    for device in greeted:
        pl.semaphore_signal(barrier, inc=1, device_id=device, device_id_type=MESH)

    own = pltpu.make_async_copy(x_hbm, xg.at[0, y], own_sem)
    own.start()
    loads = [
        pltpu.make_async_copy(src, dst, load_sem.at[i])
        for i, (src, dst) in enumerate(
            ((gain_hbm, gain), (len_hbm, lens), (fresh_hbm, fresh), (wq_hbm.at[:, core], wq.at[0]))
        )
    ]
    for load in loads:
        load.start()

    def lanes(k, parity):
        return pl.ds(pl.multiple_of((2 * k + parity) * width, width), width)

    for k in range(chips):
        pltpu.make_async_copy(
            wkv_hbm.at[:, lanes(k, core)], wkv_raw.at[k, 0], load_sem.at[4]
        ).start()
    pl.semaphore_wait(barrier, len(greeted))

    half = chips // 2
    halves = (range(0, PIECES // 2), range(PIECES // 2, PIECES))
    sides = ((0, 1), (1, -1))
    passed_by = {1: 0, 2: 0, 3: 2, 4: 2}

    def pieces(k, d):
        return range(PIECES) if k < half else halves[d]

    def pass_on(turn, k, p, d, src=None):
        sign = sides[d][1]
        owner = chip(-sign * k)
        chunk = xg.at[turn, owner, piece(p)]
        for k2 in (4, 3, 2, 1):
            if passed_by[k2] == k and k2 > k and p in pieces(k2, d):
                send(chunk if src is None else src, chunk, ring_send.at[turn],
                     ring_recv.at[turn, d, k2, p], peer(sign * (k2 - k)))

    def await_ring(turn, k):
        for p in range(PIECES):
            for d, sign in sides:
                if p in pieces(k, d):
                    await_recv(xg.at[turn, chip(-sign * k), piece(p)], ring_recv.at[turn, d, k, p])
                    pass_on(turn, k, p, d)

    def swap_weights():
        for k in range(chips):
            send(wkv_hbm.at[:, lanes(k, 1 - core)], wkv_raw.at[k, 1], swap_send.at[0],
                 swap_recv.at[0], mate)
        send(wq_hbm.at[:, 1 - core], wq.at[1], swap_send.at[1], swap_recv.at[1], mate)

    def masks():
        for load in loads[1:3]:
            load.wait()
        docs = lens.shape[1]
        lens_pad[...] = jnp.zeros_like(lens_pad)
        lens_pad[:, 0:docs] = lens[...].astype(F32)
        n = lens_pad.shape[1]
        e0, e1 = iota((n, n), 0), iota((n, n), 1)
        row = jnp.broadcast_to(lens_pad[...], (n, n))
        far = F32(1e9)
        ends_col = jnp.sum(jnp.where(e1 <= e0, row, 0.0), axis=1, keepdims=True)
        ends_col = jnp.where(iota((n, 1), 0) < docs, ends_col, far)
        ends_row = jnp.sum(jnp.where(e0 == e1, ends_col, 0.0), axis=0, keepdims=True)
        start = ((sections - 1 - s) * tokens).astype(F32)

        def docs_of_rows(begin):
            pos = begin + iota((tokens, n), 0).astype(F32)
            return jnp.sum((ends_row <= pos).astype(F32), axis=1, keepdims=True)

        def docs_of_columns(begin):
            pos = begin + iota((n, tokens), 1).astype(F32)
            return jnp.sum((ends_col <= pos).astype(F32), axis=0, keepdims=True)

        q1, q2 = docs_of_rows(start), docs_of_rows(start + tokens)
        k1, k2 = docs_of_columns(start), docs_of_columns(start + tokens)
        causal = iota((tokens, tokens), 1) <= iota((tokens, tokens), 0)
        bias1[...] = jnp.where(causal & (q1 == k1), 0.0, NEG)
        bias2[:, 0:tokens] = jnp.where(q2 == k1, 0.0, NEG)
        bias2[:, tokens:2 * tokens] = jnp.where(causal & (q2 == k2), 0.0, NEG)
    r, c = iota((columns, columns), 0), iota((columns, columns), 1)
    perm = (((c % 8) // 2 == r // 16) & (c // 8 == r % 8) & (c % 2 == (r % 16) // 8))
    perm = perm.astype(F32).astype(BF16)

    def order_columns():
        for k in range(chips):
            for side in range(2):
                wkv[k, side * columns:(side + 1) * columns] = jnp.dot(
                    perm, wkv_raw[k, side], preferred_element_type=F32
                ).astype(BF16)

    def clear():
        acc[...] = jnp.zeros_like(acc)
        sq[...] = jnp.zeros_like(sq)

    def take(turn, offset):
        k = chip(offset)
        wide = xg[turn, k].astype(F32)
        low, high = wide[:, 0:128], wide[:, 128:256]
        sq[...] += low * low + high * high
        scaled = (wide * gain[:, lanes(k, core)]).astype(BF16)
        xn[:, pl.ds(pl.multiple_of(k * width, width), width)] = scaled
        w = (wkv_quad if turn else wkv_raw)[k].reshape(2 * columns, width)
        acc[...] += lax.dot_general(w, scaled, NT, preferred_element_type=F32)

    def take_both(turn, k):
        take(turn, -k)
        if k < half:
            take(turn, k)

    group = h * here // GROUP
    sel_r, sel_c = iota((HD, 2 * HD), 0), iota((HD, 2 * HD), 1)
    same_peer = sel_r // 8 == sel_c // 16
    pick_key = (same_peer & (sel_c % 16 == sel_r % 8)).astype(F32).astype(BF16)
    pick_value = (same_peer & (sel_c % 16 == 8 + sel_r % 8)).astype(F32).astype(BF16)
    diag = iota((tokens, tokens), 0) == iota((tokens, tokens), 1)

    def share_out(act):
        part = y % half
        for m in range(KVH):
            target = 2 * m + y // half
            for side, at in ((0, core), (1, 1 - core)):
                slot = ((part // 2 + core) % 2) * 4 + (part % 2) * 2 + at
                rows_of = pl.ds(side * columns + m * 16, 16)
                act(target, wkv.at[:, rows_of], wkv_quad.at[:, slot])

    def start_share(target, src, dst):
        @pl.when(target == y)
        def _():
            pltpu.make_async_copy(src, dst, quad_recv).start()

        @pl.when(target != y)
        def _():
            send(src, dst, quad_send, quad_recv, (s, target * 2 + core))

    early = s % LINE == 0

    def share():
        order_columns()
        share_out(start_share)

    def exchange(turn):
        square = jnp.sum(sq[...], axis=1, keepdims=True)
        square = jnp.sum(jnp.where(diag, square, 0.0), axis=0, keepdims=True)
        part_out[turn, 0:columns] = acc[columns:2 * columns]
        part_out[turn, columns:columns + 8] = jnp.broadcast_to(square, (8, tokens))
        send(part_out.at[turn], part_in.at[turn], part_send.at[turn], part_recv.at[turn], mate)
        await_recv(part_in.at[turn], part_recv.at[turn])
        square = square + part_in[turn, columns:columns + 1]
        scale = lax.rsqrt(square * (1.0 / (heads * width)) + EPS)
        total = acc[0:columns] + part_in[turn, 0:columns]
        total = (total * scale).astype(BF16)
        if turn == 0:
            total = jnp.dot(perm, total, preferred_element_type=F32).astype(BF16)
        kvst[turn] = total.reshape(KVH, 16, tokens)
        if turn == 1:
            quad = h // KVH * KVH
            mine = kvbuf.at[1, pl.ds(h % KVH * KVH, KVH)]
            for d in (2, 3, 1):
                send(kvst.at[1], mine, kv_send.at[1], kv_recv.at[1], (s, quad + (h + d) % KVH))
            keep = pltpu.make_async_copy(kvst.at[1], mine, kv_own.at[1])
            keep.start()
            return scale, keep
        far_first = sorted(range(1 - half, half + 1), key=abs, reverse=True)
        others = [chip(far) * 2 + side for far in far_first if far for side in (core, 1 - core)]
        for other in others + [y * 2 + 1 - core]:
            send(kvst.at[turn, other * here // GROUP], kvbuf.at[turn, h],
                 kv_send.at[turn], kv_recv.at[turn], (s, other))
        keep = pltpu.make_async_copy(kvst.at[turn, group], kvbuf.at[turn, h], kv_own.at[turn])
        keep.start()
        return scale, keep

    def queries(turn, scale):
        def product(side):
            w = wq[side].reshape(chips * width, width)
            return jnp.dot(xn[...], w, preferred_element_type=F32)

        query_out[turn] = product(1)
        send(query_out.at[turn], query_in.at[turn], query_send.at[turn], query_recv.at[turn], mate)
        q = product(0)
        scale = jnp.sum(jnp.where(diag, scale, 0.0), axis=1, keepdims=True)
        await_recv(query_in.at[turn], query_recv.at[turn])
        q = ((q + query_in[turn]) * scale).astype(BF16)
        spread = [
            jnp.dot(q[:, i * HD:(i + 1) * HD], pick_key, preferred_element_type=F32)
            for i in range(here)
        ]
        return jnp.concatenate(spread, axis=0).astype(BF16)

    kv_count = (heads - 1, heads - KVH)

    def await_kv(turn, keep):
        keep.wait()
        await_recv(kvbuf.at[turn, pl.ds(0, kv_count[turn])], kv_recv.at[turn])

    def against(turn, wide_q):
        kv = kvbuf[turn].reshape(heads * 16, tokens)
        scores = jnp.dot(wide_q, kv, preferred_element_type=F32) * (1.0 / math.sqrt(HD))
        return scores, jnp.dot(pick_value, kv, preferred_element_type=F32).astype(BF16)

    def attend(turn, wide_q, bias, resident=()):
        both = [*resident, against(turn, wide_q)]
        values = jnp.concatenate([v for _, v in both], axis=1)
        scores = jnp.concatenate([sc for sc, _ in both], axis=1)
        scores = scores + jnp.concatenate([bias[...]] * here, axis=0)
        expon = jnp.exp(scores - jnp.max(scores, axis=1, keepdims=True))
        weights = (expon / jnp.sum(expon, axis=1, keepdims=True)).astype(BF16)
        mixed = lax.dot_general(weights, values, NT, preferred_element_type=F32).astype(BF16)
        mixed = mixed.astype(F32)
        for i in range(here):
            cols = slice(i * HD, (i + 1) * HD)
            total = xg[turn, y, :, cols].astype(F32) + mixed[i * tokens:(i + 1) * tokens]
            if turn == 0:
                total = jnp.where(s == sections - 1, fresh[:, cols].astype(F32), total)
                first[:, cols] = total.astype(BF16)
            else:
                out_ref[:, cols] = total.astype(BF16)

    def rest_of_gather(turn):
        if turn == 1:
            await_recv(wkv_quad, quad_recv)
            take(1, 0)
        await_ring(turn, 2)
        if turn == 0:
            loads[0].wait()
            pltpu.make_async_copy(wkv_raw.at[:, 0], wkv_raw.at[:, 0], load_sem.at[4]).wait()
            await_recv(wkv_raw.at[:, 1], swap_recv.at[0])
            pl.when(early)(share)
            own.wait()
            take(0, 0)
        await_ring(turn, 1)
        take_both(turn, 1)
        take_both(turn, 2)
        await_ring(turn, 3)
        take_both(turn, 3)
        await_ring(turn, 4)
        take_both(turn, 4)

    for p in range(PIECES):
        for d, _ in sides:
            pass_on(0, 0, p, d, x_hbm.at[piece(p)])
    swap_weights()
    clear()
    rest_of_gather(0)
    scale, keep = exchange(0)
    loads[3].wait()
    await_recv(wq.at[1], swap_recv.at[1])
    wide_q = queries(0, scale)
    masks()
    await_kv(0, keep)
    attend(0, wide_q, bias1)

    for p in range(PIECES):
        send(first.at[piece(p)], xg.at[1, y, piece(p)], hop_send, ring_recv.at[1, 0, 0, p], following)

    pl.when(jnp.logical_not(early))(share)

    clear()
    for p in range(PIECES):
        await_recv(xg.at[1, y, piece(p)], ring_recv.at[1, 0, 0, p])
        for d, _ in sides:
            pass_on(1, 0, p, d)
    rest_of_gather(1)
    scale, keep = exchange(1)
    wide_q = queries(1, scale)
    resident = against(0, wide_q)
    await_kv(1, keep)
    attend(1, wide_q, bias2, [resident])

    await_send(first, hop_send)
    keeps = y % 2 == y // half

    @pl.when(keeps)
    def _():
        await_send(wkv_quad.at[:, 0:2 * (KVH - 1)], quad_send)

    @pl.when(jnp.logical_not(keeps))
    def _():
        await_send(wkv_quad, quad_send)

    await_send(wkv_raw.at[:, 1], swap_send.at[0])
    await_send(wq.at[1], swap_send.at[1])
    for turn in range(2):
        await_send(xg.at[turn, pl.ds(0, 2 * half - 1)], ring_send.at[turn])
        await_send(part_out.at[turn], part_send.at[turn])
        await_send(query_out.at[turn], query_send.at[turn])
        await_send(kvbuf.at[turn, pl.ds(0, kv_count[turn])], kv_send.at[turn])


def solution(mesh):
    heads = mesh.shape["head"]
    chips = heads // 2

    def shards(entering, fresh_slice, norm_gain, w_query, w_key_value, doc_lengths):
        _, tokens, width = entering.shape
        features = w_query.shape[1]
        columns = w_key_value.shape[2]
        docs = doc_lengths.shape[0]
        any_spec = pl.BlockSpec(memory_space=pl.ANY)
        dma = pltpu.SemaphoreType.DMA
        vmem = pltpu.VMEM
        out = pl.pallas_call(
            body,
            out_shape=pltpu.VMEM((tokens, width), BF16),
            in_specs=[any_spec] * 6,
            out_specs=pl.BlockSpec(memory_space=pltpu.VMEM),
            scratch_shapes=[
                vmem((2, chips, tokens, width), BF16),
                vmem((tokens, features // 2), BF16),
                vmem((2, chips, width, width), BF16),
                vmem((chips, 2, columns, width), BF16),
                vmem((chips, 2 * columns, width), BF16),
                vmem((chips, 2 * KVH, 16, width), BF16),
                vmem((1, features), F32),
                vmem((1, docs), jnp.int32),
                vmem((1, 128), F32),
                vmem((tokens, width), BF16),
                vmem((tokens, width), BF16),
                vmem((2, KVH, 16, tokens), BF16),
                vmem((2, heads, 16, tokens), BF16),
                vmem((2 * columns, tokens), F32),
                vmem((tokens, 128), F32),
                vmem((2, columns + 8, tokens), F32),
                vmem((2, columns + 8, tokens), F32),
                vmem((2, tokens, width), F32),
                vmem((2, tokens, width), F32),
                vmem((tokens, tokens), F32),
                vmem((tokens, 2 * tokens), F32),
                dma((5,)),
                dma,
                dma((2,)),
                dma((2,)),
                dma((2, 2, 5, PIECES)),
                dma((2,)),
                dma,
                dma((2,)),
                dma((2,)),
                dma((2,)),
                dma((2,)),
                dma((2,)),
                dma((2,)),
                dma((2,)),
                dma,
                dma,
            ],
            compiler_params=pltpu.CompilerParams(collective_id=0, has_side_effects=True),
        )(
            entering[0], fresh_slice, norm_gain, w_query[0].reshape(chips, 2, width, width),
            w_key_value[0].T, doc_lengths.reshape(1, docs),
        )
        return out[None]

    placed = (
        P("section", None, "head"),
        P(None, "head"),
        P("section", None),
        P("section", None, "head"),
        P("section", None, "head"),
        P(),
    )
    return jax.shard_map(
        shards, mesh=mesh, in_specs=placed, out_specs=P("section", None, "head"), check_vma=False
    )
```
